32 devices in a mesh: member: 4 (over y, x), shard: 8 (over z, core).
Axes of the slice: x: 2, y: 2, z: 4, core: 2. Of those that a mesh axis runs over, the one named last changes fastest.
Arguments:
- trunk_out: bfloat16 [128, 8192], P('shard', 'member'), may hold values from -6 to 6
- segment_ids: int32 [128], replicated, may hold values from 0 to 7, never falling along the last dimension, each value on 1 to 32 neighbouring positions
- pair_order: int32 [8], replicated, may hold values from 0 to 7, each once
- w_query: bfloat16 [4, 8, 4096, 128], P('member', 'shard'), may hold values from -0.25 to 0.25
- w_key_value: bfloat16 [4, 8, 1024, 256], P('member', 'shard'), may hold values from -0.0625 to 0.0625
- w_out: bfloat16 [4, 512, 8192], P('member', 'shard'), may hold values from -0.25 to 0.25
- norm_gain: float32 [4, 8192], P('member'), may hold values from 0.1 to 1.9
- reward_weight: float32 [4, 8192], P('member'), may hold values from -0.0625 to 0.0625
Outputs:
- trunk_grad: float32 [128, 8192], P('member', 'shard')
- rewards: float32 [4, 8], P('member')
The draws below stay inside these ranges and needn't reach their ends.
Inputs may be any that keep to these rules, and one draw needn't show every extreme that they name: `segment_ids`: segment numbers never fall along the tokens; every sequence 0 to 7 has 1 to 32 tokens, and one has exactly 32. Each sequence appears once; sequence pair_order[2 * i] is preferred to sequence pair_order[2 * i + 1].
All inputs are finite; a program needn't handle non-finite values.
Results may differ from the reference program's by a relative error of at most 0.011.
Values may be sent and summed in bfloat16 or wider, within the bound.
No kernel may reach another device: no remote copies, remote signals or barrier semaphores. Data moves between devices by JAX's collectives and lax.ppermute only.
A program may use at most 64 MiB of HBM per device.

```python
import math
import jax
import jax.numpy as jnp
import numpy as np
from jax import lax

D = 8192
HD = 128
TOK = 128
SEG_MOST = 32
HEADS = 4
KVH = 1
QG = 4
SEQS = 8
MEMBERS = 4


def steps_of(own_key, dims, shards, least, largest):
    def one(position, parts):
        steps = jax.random.uniform(jax.random.fold_in(jax.random.fold_in(own_key, 6), position), (parts,), jnp.float32, least / len(shards), largest / len(shards))
        return jnp.repeat(jnp.exp(steps), dims[position] // parts).reshape((-1,) + (1,) * (len(dims) - position - 1))

    factor_of = one(*shards[0])
    for cut in shards[1:]:
        factor_of = factor_of * one(*cut)
    return factor_of


def profile(count, total, bound, lean):
    portions = [(1 << 20) // math.isqrt(standing ** lean) + 1 for standing in range(2, count + 1)]
    rest, holding = total - bound - (count - 1), [1] * (count - 1)
    while rest > 0:
        free = [i for i in range(count - 1) if holding[i] < bound]
        pool, left = sum([portions[i] for i in free]), rest
        for i in free:
            addition = min(bound - holding[i], max(1, left * portions[i] // pool), rest)
            holding[i] = holding[i] + addition
            rest = rest - addition
    return np.array([bound] + holding)


def ragged_sizes(rng, amount, total, bound, lean):
    if amount == 2:
        one = jax.random.randint(rng, (), max(1, total - bound), min(bound, total - 1) + 1)
        return jnp.stack([one, total - one])
    sizes = jnp.asarray(profile(amount, total, bound, lean), jnp.int32)
    twos = (amount - 1) // 2
    giver, receiver = sizes[1:1 + 2 * twos:2], sizes[2:2 + 2 * twos:2]
    room = jnp.minimum(giver - 1, bound - receiver)
    passed = jax.random.randint(jax.random.fold_in(rng, 1), (twos,), 0, 1 << 20) % (room + 1)
    sizes = sizes.at[1:1 + 2 * twos:2].set(giver - passed).at[2:2 + 2 * twos:2].set(receiver + passed)
    return sizes[jax.random.permutation(jax.random.fold_in(rng, 2), amount)]


def centred(own_key, shape, deviation, limit, cuts=(), held_as=jnp.bfloat16):
    values = deviation * jax.random.normal(own_key, shape, jnp.float32)
    if cuts:
        values = values * steps_of(own_key, shape, cuts, -0.22, 0.18)
    return jnp.clip(values, -limit, limit).astype(held_as)


def setup_inputs(seed: int = 0) -> dict:
    seeds = jax.random.split(jax.random.key(seed), 9)
    trunk_out = centred(seeds[0], (TOK, D), 1.0, 6.0, ((0, 8), (1, 4)))
    segment_ids = jnp.searchsorted(jnp.cumsum(ragged_sizes(seeds[1], SEQS, TOK, SEG_MOST, 1)), jnp.arange(TOK), side="right").astype(jnp.int32)
    pair_order = jax.random.permutation(seeds[2], SEQS).astype(jnp.int32)
    w_query = centred(seeds[3], (MEMBERS, 2 * HEADS, D // 2, HD), (D // 16) ** -0.5, 0.25, ((0, 4), (1, 8)))
    w_key_value = centred(seeds[4], (MEMBERS, 2 * HEADS, D // (2 * QG), 2 * HD), D ** -0.5, 0.0625, ((0, 4), (1, 8)))
    w_out = centred(seeds[5], (MEMBERS, HEADS * HD, D), (HEADS * HD) ** -0.5, 0.25, ((0, 4), (1, 8)))
    norm_gain = jnp.clip(1.0 + 0.18 * jax.random.normal(seeds[6], (MEMBERS, D), jnp.float32), 0.1, 1.9)
    reward_weight = centred(seeds[7], (MEMBERS, D), D ** -0.5, 0.0625, ((0, 4),), jnp.float32)
    return {"trunk_out": trunk_out, "segment_ids": segment_ids, "pair_order": pair_order, "w_query": w_query, "w_key_value": w_key_value, "w_out": w_out, "norm_gain": norm_gain, "reward_weight": reward_weight}


softcap_limit = 20.0
loss_scale = 256.0
norm_eps = 1e-05

def unfold_query(packed):
    return packed.reshape(HEADS, 2, D // 2, HD).transpose(1, 2, 0, 3).reshape(D, HEADS * HD)

def unfold_kv(portion):
    return portion.transpose(2, 1, 3, 0, 4).reshape(D, KVH * HD)

def reference(trunk_out, segment_ids, pair_order, w_query, w_key_value, w_out, norm_gain, reward_weight):
    scale_factor = 1.0 / math.sqrt(HD)
    positions = jnp.arange(TOK)
    allowed = (segment_ids[:, None] == segment_ids[None, :]) & (positions[None, :] <= positions[:, None])
    member_of = jnp.arange(SEQS)[:, None] == segment_ids[None, :]
    pooling = member_of.astype(jnp.bfloat16)
    lengths = lax.optimization_barrier(jnp.sum(member_of.astype(jnp.float32), axis=1))
    pooled_input = jnp.dot(pooling, trunk_out, preferred_element_type=jnp.float32) / lengths[:, None]
    chosen_ids = pair_order[0::2]
    rejected_ids = pair_order[1::2]

    def one_member(carry_sum, member_weights):
        query_packed, kv_packed, out_full, gain_vector, head_weight = member_weights
        query_full = unfold_query(query_packed)
        arranged = kv_packed.reshape(KVH, QG, 2, D // (2 * QG), 2 * HD)
        key_full = unfold_kv(arranged[..., :HD])
        value_full = unfold_kv(arranged[..., HD:])
        queries = jnp.dot(trunk_out, query_full, preferred_element_type=jnp.float32).astype(jnp.bfloat16).reshape(TOK, HEADS, HD)
        keys_all = jnp.dot(trunk_out, key_full, preferred_element_type=jnp.float32).astype(jnp.bfloat16).reshape(TOK, KVH, HD)
        values_all = jnp.dot(trunk_out, value_full, preferred_element_type=jnp.float32).astype(jnp.bfloat16).reshape(TOK, KVH, HD)
        key_heads = jnp.repeat(keys_all, QG, axis=1).astype(jnp.float32)
        value_heads = jnp.repeat(values_all, QG, axis=1).astype(jnp.float32)
        raw_scores = jnp.einsum('thd,shd->hts', queries.astype(jnp.float32), key_heads) * scale_factor
        capped = softcap_limit * jnp.tanh(raw_scores / softcap_limit)
        weights_exp = jnp.where(allowed[None], jnp.exp(capped), 0.0)
        attention = weights_exp / lax.optimization_barrier(jnp.sum(weights_exp, axis=2, keepdims=True))
        attention_low = attention.astype(jnp.bfloat16)
        attended = jnp.einsum('hts,shd->thd', attention_low.astype(jnp.float32), value_heads).astype(jnp.bfloat16).reshape(TOK, HEADS * HD)
        seq_mean = (jnp.dot(pooling, attended, preferred_element_type=jnp.float32) / lengths[:, None]).astype(jnp.bfloat16)
        hidden = pooled_input + jnp.dot(seq_mean, out_full, preferred_element_type=jnp.float32)
        inverse_rms = lax.rsqrt(lax.optimization_barrier(jnp.mean(hidden * hidden, axis=1)) + norm_eps)
        normed = hidden * inverse_rms[:, None] * gain_vector
        rewards = lax.optimization_barrier(jnp.sum(normed * head_weight, axis=1))
        margin = rewards[chosen_ids] - rewards[rejected_ids]
        pair_slope = loss_scale * jax.nn.sigmoid(-margin)
        reward_grad = jnp.zeros((SEQS,), jnp.float32).at[rejected_ids].add(pair_slope).at[chosen_ids].add(-pair_slope)
        scaled_grad = reward_grad[:, None] * head_weight * gain_vector
        hidden_grad = inverse_rms[:, None] * (scaled_grad - hidden * (inverse_rms ** 2)[:, None] * lax.optimization_barrier(jnp.mean(hidden * scaled_grad, axis=1, keepdims=True)))
        per_token = hidden_grad / lengths[:, None]
        mean_grad = jnp.dot(hidden_grad.astype(jnp.bfloat16), out_full.T, preferred_element_type=jnp.float32) / lengths[:, None]
        out_grad = mean_grad[segment_ids].astype(jnp.bfloat16).reshape(TOK, HEADS, HD).astype(jnp.float32)
        prob_grad = jnp.einsum('thd,shd->hts', out_grad, value_heads)
        score_grad = attention * (prob_grad - lax.optimization_barrier(jnp.sum(attention * prob_grad, axis=2, keepdims=True)))
        raw_grad = (score_grad * (1.0 - (capped / softcap_limit) ** 2) * scale_factor).astype(jnp.bfloat16).astype(jnp.float32)
        query_grad = jnp.einsum('hts,shd->thd', raw_grad, key_heads).astype(jnp.bfloat16).reshape(TOK, HEADS * HD)
        key_grad = jnp.einsum('hts,thd->shd', raw_grad, queries.astype(jnp.float32))
        key_grad = key_grad.reshape(TOK, KVH, QG, HD).sum(axis=2).astype(jnp.bfloat16).reshape(TOK, KVH * HD)
        value_grad = jnp.einsum('hts,thd->shd', attention_low.astype(jnp.float32), out_grad)
        value_grad = value_grad.reshape(TOK, KVH, QG, HD).sum(axis=2).astype(jnp.bfloat16).reshape(TOK, KVH * HD)
        member_grad = jnp.dot(query_grad, query_full.T, preferred_element_type=jnp.float32)
        member_grad = member_grad + jnp.dot(key_grad, key_full.T, preferred_element_type=jnp.float32)
        member_grad = member_grad + jnp.dot(value_grad, value_full.T, preferred_element_type=jnp.float32)
        member_grad = member_grad + per_token[segment_ids]
        return (carry_sum + member_grad, rewards)
    trunk_grad, rewards = lax.scan(one_member, jnp.zeros((TOK, D), jnp.float32), (w_query, w_key_value, w_out, norm_gain, reward_weight))
    return (trunk_grad, rewards)
```

```python
import math

import jax
import jax.numpy as jnp
from jax import lax
from jax.experimental import pallas as pl
from jax.experimental.pallas import tpu as pltpu
from jax.sharding import PartitionSpec as P

HD = 128
SEQS = 8


KERNEL_VMEM = 8 << 20
softcap_limit = 20.0
loss_scale = 256.0
norm_eps = 1e-05


def from_partner(block, axis, stride):
    count = lax.axis_size(axis)
    route = []
    for low in range(count):
        high = low | 1 << stride
        if high != low and high < count:
            route += [(low, high), (high, low)]
    return lax.ppermute(block, axis, route)


def partner_swap(values, bit_number):
    return from_partner(values, "shard", bit_number)


def group_total(values, bit_list):
    for bit_number in bit_list:
        values = values + partner_swap(values, bit_number)
    return values


def pair_join(own_part, other_part, pair_side, join_axis):
    first_part = jnp.where(pair_side == 0, own_part, other_part)
    second_part = jnp.where(pair_side == 0, other_part, own_part)
    return jnp.concatenate([first_part, second_part], axis=join_axis)


def general_device(
    trunk_out, segment_ids, pair_order, w_query, w_key_value, w_out, norm_gain, reward_weight
):
    n_shard = lax.axis_size("shard")
    query_heads = n_shard // 2
    kv_count = max(1, query_heads // 8)
    group_size = query_heads // kv_count
    shard_index = lax.axis_index("shard")
    pair_side = shard_index % 2
    head_index = shard_index // 2
    block_index = shard_index % (2 * group_size) // 2
    local_rows, local_width = trunk_out.shape
    features = lax.all_gather(trunk_out, "member", axis=1, tiled=True)
    gathered = lax.all_gather(features, "shard", axis=0, tiled=True)
    tok_count, model_width = gathered.shape
    half_width = model_width // 2
    half_rows = tok_count // 2
    half_head = HD // 2
    row_block = half_width // group_size
    scale_factor = 1.0 / math.sqrt(HD)
    group_bits = list(range((2 * group_size).bit_length() - 1))
    query_piece = w_query[0, 0]
    kv_piece = w_key_value[0, 0]
    out_rows = w_out[0]
    gain_vector = norm_gain[0]
    head_weight = reward_weight[0]
    positions = jnp.arange(tok_count)
    own_start = pair_side * half_rows
    own_positions = own_start + jnp.arange(half_rows)
    own_segments = lax.dynamic_slice_in_dim(segment_ids, own_start, half_rows, 0)
    allowed = (own_segments[:, None] == segment_ids[None, :]) & (
        positions[None, :] <= own_positions[:, None]
    )
    member_of = jnp.arange(SEQS)[:, None] == segment_ids[None, :]
    pooling = member_of.astype(jnp.bfloat16)
    lengths = jnp.sum(member_of.astype(jnp.float32), axis=1)
    own_pooling = lax.dynamic_slice_in_dim(pooling, own_start, half_rows, 1)
    half_features = lax.dynamic_slice_in_dim(gathered, pair_side * half_width, half_width, 1)
    query_partial = jnp.dot(half_features, query_piece, preferred_element_type=jnp.float32)
    kept_rows = lax.dynamic_slice_in_dim(query_partial, own_start, half_rows, 0)
    sent_rows = lax.dynamic_slice_in_dim(query_partial, half_rows - own_start, half_rows, 0)
    queries = (kept_rows + partner_swap(sent_rows, 0)).astype(jnp.bfloat16)
    kv_features = lax.dynamic_slice_in_dim(half_features, block_index * row_block, row_block, 1)
    kv_values = group_total(
        jnp.dot(kv_features, kv_piece, preferred_element_type=jnp.float32), group_bits
    ).astype(jnp.bfloat16)
    key_full = kv_values[:, :HD]
    value_full = kv_values[:, HD:]
    raw_scores = (
        jnp.einsum("td,sd->ts", queries, key_full, preferred_element_type=jnp.float32)
        * scale_factor
    )
    capped = softcap_limit * jnp.tanh(raw_scores / softcap_limit)
    weights_exp = jnp.where(allowed, jnp.exp(capped), 0.0)
    attention = weights_exp / jnp.sum(weights_exp, axis=1, keepdims=True)
    attention_low = attention.astype(jnp.bfloat16)
    attended = jnp.dot(attention_low, value_full, preferred_element_type=jnp.float32).astype(
        jnp.bfloat16
    )
    seq_part = jnp.dot(own_pooling, attended, preferred_element_type=jnp.float32)
    seq_total = seq_part + partner_swap(seq_part, 0)
    seq_mean = (seq_total / lengths[:, None]).astype(jnp.bfloat16)
    own_dims = lax.dynamic_slice_in_dim(seq_mean, pair_side * half_head, half_head, 1)
    head_part = jnp.dot(own_dims, out_rows, preferred_element_type=jnp.float32)
    pooled_attn = lax.psum(head_part, "shard")
    pooled_input = jnp.dot(pooling, gathered, preferred_element_type=jnp.float32) / lengths[:, None]
    hidden = pooled_input + pooled_attn
    inverse_rms = lax.rsqrt(jnp.mean(hidden * hidden, axis=1) + norm_eps)
    normed = hidden * inverse_rms[:, None] * gain_vector
    rewards = jnp.sum(normed * head_weight, axis=1)
    seq_ids = jnp.arange(SEQS)
    chosen = (pair_order[0::2][:, None] == seq_ids[None, :]).astype(jnp.float32)
    rejected = (pair_order[1::2][:, None] == seq_ids[None, :]).astype(jnp.float32)
    margin = jnp.sum(chosen * rewards, axis=1) - jnp.sum(rejected * rewards, axis=1)
    pair_slope = loss_scale * jax.nn.sigmoid(-margin)
    reward_grad = jnp.sum(rejected * pair_slope[:, None], axis=0) - jnp.sum(
        chosen * pair_slope[:, None], axis=0
    )
    scaled_grad = reward_grad[:, None] * head_weight * gain_vector
    hidden_grad = inverse_rms[:, None] * (
        scaled_grad
        - hidden * (inverse_rms**2)[:, None] * jnp.mean(hidden * scaled_grad, axis=1, keepdims=True)
    )
    per_token = hidden_grad / lengths[:, None]
    grad_low = hidden_grad.astype(jnp.bfloat16)
    grad_dims = (
        jnp.einsum("jd,ed->je", grad_low, out_rows, preferred_element_type=jnp.float32)
        / lengths[:, None]
    )
    mean_grad = pair_join(grad_dims, partner_swap(grad_dims, 0), pair_side, 1)
    out_grad = jnp.take(mean_grad, own_segments, axis=0).astype(jnp.bfloat16)
    prob_grad = jnp.einsum("td,sd->ts", out_grad, value_full, preferred_element_type=jnp.float32)
    score_grad = attention * (prob_grad - jnp.sum(attention * prob_grad, axis=1, keepdims=True))
    raw_grad = (score_grad * (1.0 - (capped / softcap_limit) ** 2) * scale_factor).astype(
        jnp.bfloat16
    )
    query_grad = jnp.dot(raw_grad, key_full, preferred_element_type=jnp.float32).astype(
        jnp.bfloat16
    )
    key_grad = jnp.einsum("ts,td->sd", raw_grad, queries, preferred_element_type=jnp.float32)
    value_grad = jnp.einsum(
        "ts,td->sd", attention_low, out_grad, preferred_element_type=jnp.float32
    )
    kv_grad = group_total(jnp.concatenate([key_grad, value_grad], axis=1), group_bits).astype(
        jnp.bfloat16
    )
    query_wire = lax.optimization_barrier(query_grad).astype(jnp.float32)
    query_all = pair_join(
        query_grad, partner_swap(query_wire, 0).astype(jnp.bfloat16), pair_side, 0
    )
    grad_half = jnp.einsum("td,rd->tr", query_all, query_piece, preferred_element_type=jnp.float32)
    kv_term = jnp.einsum("te,re->tr", kv_grad, kv_piece, preferred_element_type=jnp.float32)
    start_col = block_index * row_block
    grad_half = lax.dynamic_update_slice_in_dim(
        grad_half,
        lax.dynamic_slice_in_dim(grad_half, start_col, row_block, 1) + kv_term,
        start_col,
        1,
    )
    pair_rows = 2 * local_rows
    start_row = head_index * pair_rows
    pair_segments = lax.dynamic_slice_in_dim(segment_ids, start_row, pair_rows, 0)
    token_half = lax.dynamic_slice_in_dim(per_token, pair_side * half_width, half_width, 1)
    direct = jnp.take(token_half, pair_segments, axis=0)
    grad_half = lax.dynamic_update_slice_in_dim(
        grad_half,
        lax.dynamic_slice_in_dim(grad_half, start_row, pair_rows, 0) + direct,
        start_row,
        0,
    )
    by_member = lax.psum_scatter(grad_half, "member", scatter_dimension=0, tiled=True)
    member_rows = by_member.shape[0]
    placed = lax.dynamic_update_slice_in_dim(
        jnp.zeros((member_rows, model_width), jnp.float32), by_member, pair_side * half_width, 1
    )
    trunk_grad = lax.psum_scatter(placed, "shard", scatter_dimension=1, tiled=True)
    return (trunk_grad, rewards[None])


def route_pairs(target):
    pairs = []
    for member in range(4):
        for height in range(4):
            for core in range(2):
                to = target(member, height, core)
                if to is not None:
                    pairs.append((member * 8 + height * 2 + core, to[0] * 8 + to[1] * 2 + to[2]))
    return pairs


def send(block, target):
    return lax.ppermute(block, ("member", "shard"), route_pairs(target))


def core_swap(block):
    return send(block, lambda m, z, k: (m, z, 1 - k))


def matmul(left, right):
    return jnp.dot(left, right, preferred_element_type=jnp.float32)


def matmul_nt(left, right):
    return lax.dot_general(
        left, right, (((1,), (1,)), ((), ())), preferred_element_type=jnp.float32
    )


def matmul_tn(left, right):
    return lax.dot_general(
        left, right, (((0,), (0,)), ((), ())), preferred_element_type=jnp.float32
    )


def height_total(block, height, core, wire):
    sent = block.astype(wire)
    near = send(sent, lambda m, z, k: (m, z ^ (1 + k), k))
    half = jnp.where(core == 0, sent[:, :HD], sent[:, HD:])
    far = send(half, lambda m, z, k: (m, z ^ 3, k)).astype(jnp.float32)
    zero = jnp.zeros_like(far)
    spread = jnp.concatenate(
        [jnp.where(core == 0, far, zero), jnp.where(core == 0, zero, far)], axis=1
    )
    mine = jnp.where(core == 0, sent.astype(jnp.float32), 0.0) + near.astype(jnp.float32) + spread
    return mine, core_swap(mine)


def split_high_low(value):
    high = value.astype(jnp.bfloat16)
    return high, (value - high.astype(jnp.float32)).astype(jnp.bfloat16)


def iota(shape, dimension):
    return lax.broadcasted_iota(jnp.int32, shape, dimension)


def one_hot(condition):
    return condition.astype(jnp.float32).astype(jnp.bfloat16)


def pooling_of(segments):
    return one_hot(iota((SEQS, segments.shape[1]), 0) == segments)


def lengths_of(segments):
    return jnp.sum(
        (iota((SEQS, segments.shape[1]), 0) == segments).astype(jnp.float32), axis=1, keepdims=True
    )


def local_call(kernel, outputs, *operands):
    vmem = pl.BlockSpec(memory_space=pltpu.VMEM)
    smem = pl.BlockSpec(memory_space=pltpu.SMEM)
    return pl.pallas_call(
        kernel,
        out_shape=[jax.ShapeDtypeStruct(shape, dtype) for shape, dtype in outputs],
        in_specs=[smem] + [vmem] * (len(operands) - 1),
        out_specs=[vmem] * len(outputs),
        compiler_params=pltpu.CompilerParams(vmem_limit_bytes=KERNEL_VMEM),
    )(*operands)


def stack_kernel(*refs):
    pieces, out, sems = refs[:-2], refs[-2], refs[-1]
    rows = pieces[0].shape[0]
    copies = [
        pltpu.make_async_copy(ref, out.at[pl.ds(n * rows, rows), :], sems.at[n])
        for n, ref in enumerate(pieces)
    ]
    for copy in copies:
        copy.start()
    for copy in copies:
        copy.wait()


def stack_rows(blocks):
    rows, width = blocks[0].shape
    return pl.pallas_call(
        stack_kernel,
        out_shape=jax.ShapeDtypeStruct((len(blocks) * rows, width), blocks[0].dtype),
        in_specs=[pl.BlockSpec(memory_space=pl.ANY)] * len(blocks),
        out_specs=pl.BlockSpec(memory_space=pltpu.VMEM),
        scratch_shapes=[pltpu.SemaphoreType.DMA((len(blocks),))],
        compiler_params=pltpu.CompilerParams(vmem_limit_bytes=KERNEL_VMEM),
    )(*blocks)


def kv_columns_kernel(place, own, other, out):
    rows, width = own.shape[0], out.shape[1]
    start = pl.multiple_of(place[1] // 2 % 2 * width, width)
    out[:rows, :] = own[:, pl.ds(start, width)]
    out[rows:, :] = other[:, pl.ds(start, width)]


def query_kernel(place, own, other, first, second, out_first, out_second):
    rows = own.shape[0]
    for weight, out in ((first, out_first), (second, out_second)):
        out[:rows, :] = matmul(own[...], weight[...])
        out[rows:, :] = matmul(other[...], weight[...])


def token_order(place, tokens):
    height, first = place[1] // 2, place[0] // 2
    position = iota((tokens, tokens), 1)
    rows = tokens // 8
    token = (
        2 * rows * (height ^ (position // rows % 4))
        + rows * ((position // (4 * rows)) ^ first)
        + position % rows
    )
    return one_hot(iota((tokens, tokens), 0) == token)


def kv_kernel(place, segments, first, second, weight, out, pooled):
    far = (place[1] // 4) ^ (place[0] % 2)
    columns = jnp.where(far == 0, first[...], second[...])
    out[...] = matmul(columns, weight[...])
    order = token_order(place, columns.shape[0])
    rows_pool = matmul(pooling_of(segments[...]), order).astype(jnp.bfloat16)
    pooled[...] = matmul(rows_pool, columns) / lengths_of(segments[...])


def order_kernel(place, first, second, kv, out):
    order = token_order(place, first.shape[0])
    for value, start in ((first[...] + second[...], 0), (kv[...], HD)):
        high, low = split_high_low(value)
        out[:, start : start + value.shape[1]] = matmul(order, high) + matmul(order, low)


def forward_kernel(
    place, segments, mine, swapped, kv_mine, kv_swapped, pooled, out_own, out_other, gain,
    queries_out, kv_out, attention_out, capped_out, message,
):
    bf16 = jnp.bfloat16
    core, height = place[1] % 2, place[1] // 2
    queries = (mine[:, :HD] + swapped[:, :HD]).astype(bf16)
    kv_values = (kv_mine[...] + kv_swapped[...]).astype(bf16)
    queries_out[...] = queries
    kv_out[...] = kv_values
    keys, values = kv_values[:, :HD], kv_values[:, HD:]
    pooling = pooling_of(segments[...])
    lengths = lengths_of(segments[...])
    tokens = pooling.shape[1]
    same = matmul_tn(pooling, pooling) > 0.5
    allowed = same & (iota((tokens, tokens), 1) <= iota((tokens, tokens), 0))
    raw_scores = matmul_nt(queries, keys) * (1.0 / math.sqrt(HD))
    capped = softcap_limit * jnp.tanh(raw_scores / softcap_limit)
    weights_exp = jnp.where(allowed, jnp.exp(capped), 0.0)
    attention = weights_exp / jnp.sum(weights_exp, axis=1, keepdims=True)
    attention_out[...] = attention
    capped_out[...] = capped
    attended = matmul(attention.astype(bf16), values).astype(bf16)
    seq_mean = (matmul(pooling, attended) / lengths).astype(bf16)
    half = out_own.shape[0]
    low, high = seq_mean[:, :half], seq_mean[:, half:]
    part = matmul(jnp.where(core == 0, low, high), out_own[...]) + matmul(
        jnp.where(core == 0, high, low), out_other[...]
    )
    width = pooled.shape[1]
    part = jnp.concatenate(
        [
            part[:, n * width : (n + 1) * width] + jnp.where(height == n, pooled[...], 0.0)
            for n in range(part.shape[1] // width)
        ],
        axis=1,
    )
    product_high, product_low = split_high_low(jnp.sum(part * gain[...], axis=1, keepdims=True))
    lane = iota((SEQS, HD), 1)
    message[:, : part.shape[1]] = part.astype(bf16)
    message[:, part.shape[1] :] = jnp.where(
        lane == 0,
        product_high.astype(jnp.float32),
        jnp.where(lane == 1, product_low.astype(jnp.float32), 0.0),
    ).astype(bf16)


def stats_kernel(
    place, first, second, third, fourth, out_own, out_other, gain, hidden_out, report
):
    core = place[1] % 2
    half_width = hidden_out.shape[1]
    f32 = jnp.float32
    total = (first[...].astype(f32) + second[...].astype(f32)) + (
        third[...].astype(f32) + fourth[...].astype(f32)
    )
    hidden = total[:, :half_width]
    hidden_out[...] = hidden
    stacked = jnp.concatenate([hidden, jnp.broadcast_to(gain[...], hidden.shape)], axis=0)
    stacked = stacked.astype(jnp.bfloat16)
    along_own = matmul_nt(stacked, out_own[...])
    along_other = matmul_nt(stacked, out_other[...])
    half = along_own.shape[1]
    report[: 2 * SEQS, :half] = jnp.where(core == 0, along_own, along_other)
    report[: 2 * SEQS, half:] = jnp.where(core == 0, along_other, along_own)
    squares = jnp.sum(hidden * hidden, axis=1, keepdims=True)
    products = total[:, half_width : half_width + 1] + total[:, half_width + 1 : half_width + 2]
    lane = iota((SEQS, HD), 1)
    report[2 * SEQS :, :] = jnp.where(lane == 0, squares, jnp.where(lane == 1, products, 0.0))


def member_order(place, tokens):
    rows = tokens // 4
    position = iota((tokens, tokens), 0)
    token = rows * (place[0] ^ (position // rows)) + position % rows
    return one_hot(iota((tokens, tokens), 1) == token)


def backward_kernel(
    place, pairs, segments, mine, swapped, queries, kv_values, attention, capped,
    query_grad, kv_grad, rewards_out, factors,
):
    bf16, f32 = jnp.bfloat16, jnp.float32
    width = place[2].astype(f32)
    report = mine[...] + swapped[...]
    hidden_along, gain_along = report[:SEQS], report[SEQS : 2 * SEQS]
    square_sum, product_sum = report[2 * SEQS :, 0:1], report[2 * SEQS :, 1:2]
    pooling = pooling_of(segments[...])
    lengths = lengths_of(segments[...])
    inverse_rms = lax.rsqrt(square_sum / width + norm_eps)
    rewards = product_sum * inverse_rms
    diagonal = iota((SEQS, SEQS), 0) == iota((SEQS, SEQS), 1)
    rewards_row = jnp.sum(jnp.where(diagonal, rewards, 0.0), axis=0, keepdims=True)
    rewards_out[...] = rewards_row
    signs = pairs[...]
    margin = jnp.sum(signs * rewards_row, axis=1, keepdims=True)
    pair_slope = loss_scale / (1.0 + jnp.exp(margin))
    grad_row = -jnp.sum(signs * pair_slope, axis=0, keepdims=True)
    reward_grad = jnp.sum(jnp.where(diagonal, grad_row, 0.0), axis=1, keepdims=True)
    gain_factor = inverse_rms * reward_grad / lengths
    hidden_factor = inverse_rms * inverse_rms * inverse_rms * (
        reward_grad * product_sum / width
    ) / lengths
    factors[0] = jnp.broadcast_to(gain_factor, (SEQS, HD))
    factors[1] = jnp.broadcast_to(hidden_factor, (SEQS, HD))
    mean_grad = (gain_factor * gain_along - hidden_factor * hidden_along).astype(bf16)
    out_grad = matmul_tn(pooling, mean_grad).astype(bf16)
    keys, values = kv_values[:, :HD], kv_values[:, HD:]
    attn = attention[...]
    prob_grad = matmul_nt(out_grad, values)
    score_grad = attn * (prob_grad - jnp.sum(attn * prob_grad, axis=1, keepdims=True))
    ratio = capped[...] / softcap_limit
    raw_grad = (score_grad * (1.0 - ratio * ratio) * (1.0 / math.sqrt(HD))).astype(bf16)
    order = member_order(place, attn.shape[0])
    query_grad[...] = matmul(order, matmul(raw_grad, keys).astype(bf16)).astype(bf16)
    kv_grad[:, :HD] = matmul_tn(raw_grad, queries[...])
    kv_grad[:, HD:] = matmul_tn(attn.astype(bf16), out_grad)


def far_kernel(place, grad, weight, far):
    width = far.shape[1] // 3
    for step in (1, 2, 3):
        start = pl.multiple_of(((place[1] // 2) ^ step) * width, width)
        far[:, (step - 1) * width : step * width] = matmul_nt(
            grad[...], weight[pl.ds(start, width), :]
        ).astype(far.dtype)


def near_kernel(
    place, segments, grad, weight, kv_mine, kv_swapped, kv_weight, hidden, gain, factors, near
):
    bf16 = jnp.bfloat16
    width = near.shape[1]
    start = pl.multiple_of(place[1] // 2 * width, width)
    order = member_order(place, near.shape[0])
    kv_grad = (kv_mine[...] + kv_swapped[...]).astype(bf16)
    kv_turned = matmul(order, kv_grad).astype(bf16)
    seq_turned = matmul_nt(order, pooling_of(segments[...])).astype(bf16)
    gain_block = gain[:, pl.ds(start, width)]
    high, low = split_high_low(
        factors[0][:, 0:1] * gain_block - factors[1][:, 0:1] * hidden[:, pl.ds(start, width)]
    )
    near[...] = (
        matmul_nt(grad[...], weight[pl.ds(start, width), :])
        + matmul_nt(kv_turned, kv_weight[...])
        + matmul(seq_turned, high)
        + matmul(seq_turned, low)
    ).astype(bf16)


def member_sum_kernel(place, own, first, second, third, out):
    f32 = jnp.float32
    rows = out.shape[0]
    out[...] = (
        (own[:rows, :].astype(f32) + first[...].astype(f32))
        + (second[...].astype(f32) + third[...].astype(f32))
    ).astype(out.dtype)


def fast_device(
    trunk_out, segment_ids, pair_order, w_query, w_key_value, w_out, norm_gain, reward_weight
):
    bf16, f32 = jnp.bfloat16, jnp.float32
    member = lax.axis_index("member")
    shard = lax.axis_index("shard")
    height = shard // 2
    core = shard % 2
    col = member % 2
    local_width = trunk_out.shape[1]
    tokens = segment_ids.shape[0]
    half_width = w_query.shape[2]
    block_width = w_key_value.shape[2]
    member_rows = tokens // 4
    query_piece = w_query[0, 0]
    kv_piece = w_key_value[0, 0]
    place = jnp.stack([member, shard, jnp.int32(2 * half_width)])
    segments = segment_ids[None, :]

    stack = [trunk_out] + [
        send(trunk_out, lambda m, z, k, d=d: (m, z ^ d, k)) for d in (1, 2, 3)
    ]

    weights = [
        send(
            lax.dynamic_slice_in_dim(query_piece, (col ^ r) * local_width, local_width, 0),
            lambda m, z, k, r=r: (2 * k + ((m % 2) ^ r), z, m // 2),
        )
        for r in (0, 1)
    ]

    column_own = stack_rows(stack)
    column_other = core_swap(column_own)
    block_shape = ((tokens, block_width), bf16)
    (kv_sent,) = local_call(kv_columns_kernel, [block_shape], place, column_own, column_other)
    kv_got = [
        send(
            kv_sent,
            lambda m, z, k, r=r: (2 * k + ((m % 2) ^ r), z, m // 2) if m % 2 == z // 2 else None,
        )
        for r in (0, 1)
    ]
    head_shape = ((tokens, HD), f32)
    query_parts = local_call(
        query_kernel, [head_shape] * 2, place, column_own, column_other, *weights
    )
    query_got = [
        send(part, lambda m, z, k, r=r: (2 * k + ((m % 2) ^ r), z, m // 2))
        for r, part in enumerate(query_parts)
    ]
    kv_part, pooled = local_call(
        kv_kernel,
        [((tokens, 2 * HD), f32), ((SEQS, block_width), f32)],
        place,
        segments,
        *kv_got,
        kv_piece,
    )
    (mixed,) = local_call(
        order_kernel, [((tokens, 3 * HD), f32)], place, *query_got, kv_part
    )
    swapped = core_swap(mixed)
    kv_mine, kv_swapped = height_total(mixed[:, HD:] + swapped[:, HD:], height, core, f32)

    out_rows, _ = lax.optimization_barrier((w_out[0], mixed))
    out_own = lax.dynamic_slice_in_dim(out_rows, core * half_width, half_width, 1)
    out_other = core_swap(
        lax.dynamic_slice_in_dim(out_rows, (1 - core) * half_width, half_width, 1)
    )
    gain = lax.dynamic_slice_in_dim(
        norm_gain * reward_weight, core * half_width, half_width, 1
    )

    queries, kv_values, attention, capped, message = local_call(
        forward_kernel,
        [
            ((tokens, HD), bf16),
            ((tokens, 2 * HD), bf16),
            ((tokens, tokens), f32),
            ((tokens, tokens), f32),
            ((SEQS, half_width + HD), bf16),
        ],
        place, segments, mixed, swapped, kv_mine, kv_swapped, pooled, out_own, out_other, gain,
    )
    others = [send(message, lambda m, z, k, d=d: (m, z ^ d, k)) for d in (1, 2, 3)]
    hidden, report = local_call(
        stats_kernel,
        [((SEQS, half_width), f32), ((3 * SEQS, HD), f32)],
        place, message, *others, out_own, out_other, gain,
    )
    seq_ids = jnp.arange(SEQS)[None, :]
    pairs = (pair_order[0::2][:, None] == seq_ids).astype(f32) - (
        pair_order[1::2][:, None] == seq_ids
    ).astype(f32)
    pairs = jnp.concatenate([pairs, jnp.zeros_like(pairs)], axis=0)
    query_grad, kv_grad, rewards, factors = local_call(
        backward_kernel,
        [
            ((tokens, HD), bf16),
            ((tokens, 2 * HD), f32),
            ((1, SEQS), f32),
            ((2, SEQS, HD), f32),
        ],
        place, pairs, segments, report, core_swap(report), queries, kv_values, attention, capped,
    )

    kv_mine, kv_swapped = height_total(kv_grad, height, core, bf16)
    (far_grad,) = local_call(
        far_kernel, [((tokens, 3 * block_width), bf16)], place, query_grad, query_piece
    )
    far_got = [
        send(far_grad[d * member_rows : (d + 1) * member_rows], lambda m, z, k, d=d: (m ^ d, z, k))
        for d in (1, 2, 3)
    ]
    (near_grad,) = local_call(
        near_kernel,
        [block_shape],
        place, segments, query_grad, query_piece, kv_mine, kv_swapped, kv_piece, hidden, gain,
        factors,
    )
    near_got = [
        send(near_grad[d * member_rows : (d + 1) * member_rows], lambda m, z, k, d=d: (m ^ d, z, k))
        for d in (1, 2, 3)
    ]
    (far_sum,) = local_call(
        member_sum_kernel, [((member_rows, 3 * block_width), bf16)], place, far_grad, *far_got
    )
    (near_sum,) = local_call(
        member_sum_kernel, [((member_rows, block_width), bf16)], place, near_grad, *near_got
    )
    pieces = [near_sum] + [far_sum[:, e * block_width : (e + 1) * block_width] for e in range(3)]
    total = 0.0
    for d in (1, 2, 3, 0):
        got = send(
            pieces[d], lambda m, z, k, d=d: (m, (4 * k + (z ^ d)) // 2, z % 2 ^ d % 2)
        )
        total = total + got.astype(f32)
    return (total, rewards)


def solution(mesh):
    on_device = fast_device if dict(mesh.shape) == {"member": 4, "shard": 8} else general_device
    placed = (
        P("shard", "member"),
        P(),
        P(),
        P("member", "shard", None, None),
        P("member", "shard", None, None),
        P("member", "shard", None),
        P("member", None),
        P("member", None),
    )
    return jax.shard_map(
        on_device,
        mesh=mesh,
        in_specs=placed,
        out_specs=(P("member", "shard"), P("member", None)),
        check_vma=False,
    )
```

```python
import math

import jax
import jax.numpy as jnp
from jax import lax
from jax.experimental import pallas as pl
from jax.experimental.pallas import tpu as pltpu
from jax.sharding import PartitionSpec as P


HD = 128
SEQS = 8


KERNEL_VMEM = 8 << 20
softcap_limit = 20.0
loss_scale = 256.0
norm_eps = 1e-05


def from_partner(block, axis, stride):
    count = lax.axis_size(axis)
    route = []
    for low in range(count):
        high = low | 1 << stride
        if high != low and high < count:
            route += [(low, high), (high, low)]
    return lax.ppermute(block, axis, route)


def partner_swap(values, bit_number):
    return from_partner(values, "shard", bit_number)


def group_total(values, bit_list):
    for bit_number in bit_list:
        values = values + partner_swap(values, bit_number)
    return values


def pair_join(own_part, other_part, pair_side, join_axis):
    first_part = jnp.where(pair_side == 0, own_part, other_part)
    second_part = jnp.where(pair_side == 0, other_part, own_part)
    return jnp.concatenate([first_part, second_part], axis=join_axis)


def general_device(
    trunk_out, segment_ids, pair_order, w_query, w_key_value, w_out, norm_gain, reward_weight
):
    n_shard = lax.axis_size("shard")
    query_heads = n_shard // 2
    kv_count = max(1, query_heads // 8)
    group_size = query_heads // kv_count
    shard_index = lax.axis_index("shard")
    pair_side = shard_index % 2
    head_index = shard_index // 2
    block_index = shard_index % (2 * group_size) // 2
    local_rows, _ = trunk_out.shape
    features = lax.all_gather(trunk_out, "member", axis=1, tiled=True)
    gathered = lax.all_gather(features, "shard", axis=0, tiled=True)
    tok_count, model_width = gathered.shape
    half_width = model_width // 2
    half_rows = tok_count // 2
    half_head = HD // 2
    row_block = half_width // group_size
    scale_factor = 1.0 / math.sqrt(HD)
    group_bits = list(range((2 * group_size).bit_length() - 1))
    query_piece = w_query[0, 0]
    kv_piece = w_key_value[0, 0]
    out_rows = w_out[0]
    gain_vector = norm_gain[0]
    head_weight = reward_weight[0]
    positions = jnp.arange(tok_count)
    own_start = pair_side * half_rows
    own_positions = own_start + jnp.arange(half_rows)
    own_segments = lax.dynamic_slice_in_dim(segment_ids, own_start, half_rows, 0)
    allowed = (own_segments[:, None] == segment_ids[None, :]) & (
        positions[None, :] <= own_positions[:, None]
    )
    member_of = jnp.arange(SEQS)[:, None] == segment_ids[None, :]
    pooling = member_of.astype(jnp.bfloat16)
    lengths = jnp.sum(member_of.astype(jnp.float32), axis=1)
    own_pooling = lax.dynamic_slice_in_dim(pooling, own_start, half_rows, 1)
    half_features = lax.dynamic_slice_in_dim(gathered, pair_side * half_width, half_width, 1)
    query_partial = jnp.dot(half_features, query_piece, preferred_element_type=jnp.float32)
    kept_rows = lax.dynamic_slice_in_dim(query_partial, own_start, half_rows, 0)
    sent_rows = lax.dynamic_slice_in_dim(query_partial, half_rows - own_start, half_rows, 0)
    queries = (kept_rows + partner_swap(sent_rows, 0)).astype(jnp.bfloat16)
    kv_features = lax.dynamic_slice_in_dim(half_features, block_index * row_block, row_block, 1)
    kv_values = group_total(
        jnp.dot(kv_features, kv_piece, preferred_element_type=jnp.float32), group_bits
    ).astype(jnp.bfloat16)
    key_full = kv_values[:, :HD]
    value_full = kv_values[:, HD:]
    raw_scores = (
        jnp.einsum("td,sd->ts", queries, key_full, preferred_element_type=jnp.float32)
        * scale_factor
    )
    capped = softcap_limit * jnp.tanh(raw_scores / softcap_limit)
    weights_exp = jnp.where(allowed, jnp.exp(capped), 0.0)
    attention = weights_exp / jnp.sum(weights_exp, axis=1, keepdims=True)
    attention_low = attention.astype(jnp.bfloat16)
    attended = jnp.dot(attention_low, value_full, preferred_element_type=jnp.float32).astype(
        jnp.bfloat16
    )
    seq_part = jnp.dot(own_pooling, attended, preferred_element_type=jnp.float32)
    seq_total = seq_part + partner_swap(seq_part, 0)
    seq_mean = (seq_total / lengths[:, None]).astype(jnp.bfloat16)
    own_dims = lax.dynamic_slice_in_dim(seq_mean, pair_side * half_head, half_head, 1)
    head_part = jnp.dot(own_dims, out_rows, preferred_element_type=jnp.float32)
    pooled_attn = lax.psum(head_part, "shard")
    pooled_input = jnp.dot(pooling, gathered, preferred_element_type=jnp.float32) / lengths[:, None]
    hidden = pooled_input + pooled_attn
    inverse_rms = lax.rsqrt(jnp.mean(hidden * hidden, axis=1) + norm_eps)
    normed = hidden * inverse_rms[:, None] * gain_vector
    rewards = jnp.sum(normed * head_weight, axis=1)
    seq_ids = jnp.arange(SEQS)
    chosen = (pair_order[0::2][:, None] == seq_ids[None, :]).astype(jnp.float32)
    rejected = (pair_order[1::2][:, None] == seq_ids[None, :]).astype(jnp.float32)
    margin = jnp.sum(chosen * rewards, axis=1) - jnp.sum(rejected * rewards, axis=1)
    pair_slope = loss_scale * jax.nn.sigmoid(-margin)
    reward_grad = jnp.sum(rejected * pair_slope[:, None], axis=0) - jnp.sum(
        chosen * pair_slope[:, None], axis=0
    )
    scaled_grad = reward_grad[:, None] * head_weight * gain_vector
    hidden_grad = inverse_rms[:, None] * (
        scaled_grad
        - hidden * (inverse_rms**2)[:, None] * jnp.mean(hidden * scaled_grad, axis=1, keepdims=True)
    )
    per_token = hidden_grad / lengths[:, None]
    grad_low = hidden_grad.astype(jnp.bfloat16)
    grad_dims = (
        jnp.einsum("jd,ed->je", grad_low, out_rows, preferred_element_type=jnp.float32)
        / lengths[:, None]
    )
    mean_grad = pair_join(grad_dims, partner_swap(grad_dims, 0), pair_side, 1)
    out_grad = jnp.take(mean_grad, own_segments, axis=0).astype(jnp.bfloat16)
    prob_grad = jnp.einsum("td,sd->ts", out_grad, value_full, preferred_element_type=jnp.float32)
    score_grad = attention * (prob_grad - jnp.sum(attention * prob_grad, axis=1, keepdims=True))
    raw_grad = (score_grad * (1.0 - (capped / softcap_limit) ** 2) * scale_factor).astype(
        jnp.bfloat16
    )
    query_grad = jnp.dot(raw_grad, key_full, preferred_element_type=jnp.float32).astype(
        jnp.bfloat16
    )
    key_grad = jnp.einsum("ts,td->sd", raw_grad, queries, preferred_element_type=jnp.float32)
    value_grad = jnp.einsum(
        "ts,td->sd", attention_low, out_grad, preferred_element_type=jnp.float32
    )
    kv_grad = group_total(jnp.concatenate([key_grad, value_grad], axis=1), group_bits).astype(
        jnp.bfloat16
    )
    query_wire = lax.optimization_barrier(query_grad).astype(jnp.float32)
    query_all = pair_join(
        query_grad, partner_swap(query_wire, 0).astype(jnp.bfloat16), pair_side, 0
    )
    grad_half = jnp.einsum("td,rd->tr", query_all, query_piece, preferred_element_type=jnp.float32)
    kv_term = jnp.einsum("te,re->tr", kv_grad, kv_piece, preferred_element_type=jnp.float32)
    start_col = block_index * row_block
    grad_half = lax.dynamic_update_slice_in_dim(
        grad_half,
        lax.dynamic_slice_in_dim(grad_half, start_col, row_block, 1) + kv_term,
        start_col,
        1,
    )
    pair_rows = 2 * local_rows
    start_row = head_index * pair_rows
    pair_segments = lax.dynamic_slice_in_dim(segment_ids, start_row, pair_rows, 0)
    token_half = lax.dynamic_slice_in_dim(per_token, pair_side * half_width, half_width, 1)
    direct = jnp.take(token_half, pair_segments, axis=0)
    grad_half = lax.dynamic_update_slice_in_dim(
        grad_half,
        lax.dynamic_slice_in_dim(grad_half, start_row, pair_rows, 0) + direct,
        start_row,
        0,
    )
    by_member = lax.psum_scatter(grad_half, "member", scatter_dimension=0, tiled=True)
    member_rows = by_member.shape[0]
    placed = lax.dynamic_update_slice_in_dim(
        jnp.zeros((member_rows, model_width), jnp.float32), by_member, pair_side * half_width, 1
    )
    trunk_grad = lax.psum_scatter(placed, "shard", scatter_dimension=1, tiled=True)
    return (trunk_grad, rewards[None])


def route_pairs(target):
    pairs = []
    for member in range(4):
        for height in range(4):
            for core in range(2):
                to = target(member, height, core)
                if to is not None:
                    pairs.append((member * 8 + height * 2 + core, to[0] * 8 + to[1] * 2 + to[2]))
    return pairs


def send(block, target):
    return lax.ppermute(block, ("member", "shard"), route_pairs(target))


def core_swap(block):
    return send(block, lambda m, z, k: (m, z, 1 - k))


def matmul(left, right):
    return jnp.dot(left, right, preferred_element_type=jnp.float32)


def matmul_nt(left, right):
    return lax.dot_general(
        left, right, (((1,), (1,)), ((), ())), preferred_element_type=jnp.float32
    )


def matmul_tn(left, right):
    return lax.dot_general(
        left, right, (((0,), (0,)), ((), ())), preferred_element_type=jnp.float32
    )


def height_total(block, core, wire):
    sent = block.astype(wire)
    near = send(sent, lambda m, z, k: (m, z ^ (1 + k), k))
    half = jnp.where(core == 0, sent[:, :HD], sent[:, HD:])
    far = send(half, lambda m, z, k: (m, z ^ 3, k)).astype(jnp.float32)
    zero = jnp.zeros_like(far)
    spread = jnp.concatenate(
        [jnp.where(core == 0, far, zero), jnp.where(core == 0, zero, far)], axis=1
    )
    mine = jnp.where(core == 0, sent.astype(jnp.float32), 0.0) + near.astype(jnp.float32) + spread
    return mine, core_swap(mine)


def split_high_low(value):
    high = value.astype(jnp.bfloat16)
    return high, (value - high.astype(jnp.float32)).astype(jnp.bfloat16)


def iota(shape, dimension):
    return lax.broadcasted_iota(jnp.int32, shape, dimension)


def one_hot(condition):
    return condition.astype(jnp.float32).astype(jnp.bfloat16)


def pooling_of(segments):
    return one_hot(iota((SEQS, segments.shape[1]), 0) == segments)


def lengths_of(segments):
    return jnp.sum(
        (iota((SEQS, segments.shape[1]), 0) == segments).astype(jnp.float32), axis=1, keepdims=True
    )


def local_call(kernel, outputs, *operands):
    vmem = pl.BlockSpec(memory_space=pltpu.VMEM)
    smem = pl.BlockSpec(memory_space=pltpu.SMEM)
    return pl.pallas_call(
        kernel,
        out_shape=[jax.ShapeDtypeStruct(shape, dtype) for shape, dtype in outputs],
        in_specs=[smem] + [vmem] * (len(operands) - 1),
        out_specs=[vmem] * len(outputs),
        compiler_params=pltpu.CompilerParams(vmem_limit_bytes=KERNEL_VMEM),
    )(*operands)


def prepare_kernel(
    place, segment_ids, norm_gain, reward_weight, weight,
    segments_out, gain_out, weight_out, head_weight, sems,
):
    width = gain_out.shape[1]
    start = pl.multiple_of(place[1] % 2 * width, width)
    copies = [
        pltpu.make_async_copy(weight, weight_out, sems.at[0]),
        pltpu.make_async_copy(segment_ids, segments_out, sems.at[1]),
        pltpu.make_async_copy(norm_gain.at[:, pl.ds(start, width)], gain_out, sems.at[2]),
        pltpu.make_async_copy(reward_weight.at[:, pl.ds(start, width)], head_weight, sems.at[3]),
    ]
    for copy in copies:
        copy.start()
    for copy in copies:
        copy.wait()
    gain_out[...] = gain_out[...] * head_weight[...]


def prepare(place, segments, norm_gain, reward_weight, weight):
    width = norm_gain.shape[1] // 2
    return pl.pallas_call(
        prepare_kernel,
        out_shape=[
            jax.ShapeDtypeStruct(segments.shape, segments.dtype),
            jax.ShapeDtypeStruct((1, width), norm_gain.dtype),
            jax.ShapeDtypeStruct(weight.shape, weight.dtype),
        ],
        in_specs=[pl.BlockSpec(memory_space=pltpu.SMEM)]
        + [pl.BlockSpec(memory_space=pl.ANY)] * 4,
        out_specs=[pl.BlockSpec(memory_space=pltpu.VMEM)] * 3,
        scratch_shapes=[
            pltpu.VMEM((1, width), reward_weight.dtype),
            pltpu.SemaphoreType.DMA((4,)),
        ],
        compiler_params=pltpu.CompilerParams(vmem_limit_bytes=KERNEL_VMEM),
    )(place, segments, norm_gain, reward_weight, weight)


def stack_kernel(place, *refs):
    pieces, out, sems = refs[:-2], refs[-2], refs[-1]
    rows = pieces[0].shape[0]
    copies = []
    for step, ref in enumerate(pieces):
        start = pl.multiple_of(((place[1] // 2) ^ step) * rows, rows)
        copies.append(pltpu.make_async_copy(ref, out.at[pl.ds(start, rows), :], sems.at[step]))
    for copy in copies:
        copy.start()
    for copy in copies:
        copy.wait()


def stack_rows(place, blocks):
    rows, width = blocks[0].shape
    return pl.pallas_call(
        stack_kernel,
        out_shape=jax.ShapeDtypeStruct((len(blocks) * rows, width), blocks[0].dtype),
        in_specs=[pl.BlockSpec(memory_space=pltpu.SMEM)]
        + [pl.BlockSpec(memory_space=pl.ANY)] * len(blocks),
        out_specs=pl.BlockSpec(memory_space=pltpu.VMEM),
        scratch_shapes=[pltpu.SemaphoreType.DMA((len(blocks),))],
        compiler_params=pltpu.CompilerParams(vmem_limit_bytes=KERNEL_VMEM),
    )(place, *blocks)


def kv_columns_kernel(place, own, other, out):
    width = out.shape[1]
    rows = own.shape[0] // 4
    core = place[1] % 2
    start = pl.multiple_of(place[1] // 2 % 2 * width, width)
    for source, side in ((own, core), (other, 1 - core)):
        for step in range(4):
            to = pl.multiple_of((2 * step + side) * rows, rows)
            out[pl.ds(to, rows), :] = source[step * rows : (step + 1) * rows, pl.ds(start, width)]


def query_kernel(place, own, other, first, second, out_first, out_second):
    rows = own.shape[0] // 4
    core = place[1] % 2
    for weight, out in ((first, out_first), (second, out_second)):
        for source, side in ((own, core), (other, 1 - core)):
            part = matmul(source[...], weight[...])
            for step in range(4):
                to = pl.multiple_of((2 * step + side) * rows, rows)
                out[pl.ds(to, rows), :] = part[step * rows : (step + 1) * rows]


def kv_kernel(place, segments, first, second, weight, out, pooled):
    far = (place[1] // 4) ^ (place[0] % 2)
    columns = jnp.where(far == 0, first[...], second[...])
    out[...] = matmul(columns, weight[...])
    pooled[...] = matmul(pooling_of(segments[...]), columns) / lengths_of(segments[...])


def forward_kernel(
    place, segments, mine, swapped, kv_mine, kv_swapped, pooled, out_own, out_other, gain,
    queries_out, kv_out, attention_out, capped_out, message,
):
    bf16 = jnp.bfloat16
    core, height = place[1] % 2, place[1] // 2
    queries = (mine[:, :HD] + swapped[:, :HD]).astype(bf16)
    kv_values = (kv_mine[...] + kv_swapped[...]).astype(bf16)
    queries_out[...] = queries
    kv_out[...] = kv_values
    keys, values = kv_values[:, :HD], kv_values[:, HD:]
    pooling = pooling_of(segments[...])
    lengths = lengths_of(segments[...])
    tokens = pooling.shape[1]
    same = matmul_tn(pooling, pooling) > 0.5
    allowed = same & (iota((tokens, tokens), 1) <= iota((tokens, tokens), 0))
    raw_scores = matmul_nt(queries, keys) * (1.0 / math.sqrt(HD))
    capped = softcap_limit * jnp.tanh(raw_scores / softcap_limit)
    weights_exp = jnp.where(allowed, jnp.exp(capped), 0.0)
    attention = weights_exp / jnp.sum(weights_exp, axis=1, keepdims=True)
    attention_out[...] = attention
    capped_out[...] = capped
    attended = matmul(attention.astype(bf16), values).astype(bf16)
    seq_mean = (matmul(pooling, attended) / lengths).astype(bf16)
    half = out_own.shape[0]
    low, high = seq_mean[:, :half], seq_mean[:, half:]
    part = matmul(jnp.where(core == 0, low, high), out_own[...]) + matmul(
        jnp.where(core == 0, high, low), out_other[...]
    )
    width = pooled.shape[1]
    part = jnp.concatenate(
        [
            part[:, n * width : (n + 1) * width] + jnp.where(height == n, pooled[...], 0.0)
            for n in range(part.shape[1] // width)
        ],
        axis=1,
    )
    product_high, product_low = split_high_low(jnp.sum(part * gain[...], axis=1, keepdims=True))
    lane = iota((SEQS, HD), 1)
    message[:, : part.shape[1]] = part.astype(bf16)
    message[:, part.shape[1] :] = jnp.where(
        lane == 0,
        product_high.astype(jnp.float32),
        jnp.where(lane == 1, product_low.astype(jnp.float32), 0.0),
    ).astype(bf16)


def stats_kernel(
    place, first, second, third, fourth, out_own, out_other, gain, hidden_out, report
):
    core = place[1] % 2
    half_width = hidden_out.shape[1]
    f32 = jnp.float32
    total = (first[...].astype(f32) + second[...].astype(f32)) + (
        third[...].astype(f32) + fourth[...].astype(f32)
    )
    hidden = total[:, :half_width]
    hidden_out[...] = hidden
    stacked = jnp.concatenate([hidden, jnp.broadcast_to(gain[...], hidden.shape)], axis=0)
    stacked = stacked.astype(jnp.bfloat16)
    along_own = matmul_nt(stacked, out_own[...])
    along_other = matmul_nt(stacked, out_other[...])
    half = along_own.shape[1]
    report[: 2 * SEQS, :half] = jnp.where(core == 0, along_own, along_other)
    report[: 2 * SEQS, half:] = jnp.where(core == 0, along_other, along_own)
    squares = jnp.sum(hidden * hidden, axis=1, keepdims=True)
    products = total[:, half_width : half_width + 1] + total[:, half_width + 1 : half_width + 2]
    lane = iota((SEQS, HD), 1)
    report[2 * SEQS :, :] = jnp.where(lane == 0, squares, jnp.where(lane == 1, products, 0.0))


def member_order(place, tokens):
    rows = tokens // 4
    position = iota((tokens, tokens), 0)
    token = rows * (place[0] ^ (position // rows)) + position % rows
    return one_hot(iota((tokens, tokens), 1) == token)


def backward_kernel(
    place, pairs, segments, mine, swapped, queries, kv_values, attention, capped,
    query_grad, kv_grad, rewards_out, factors,
):
    bf16, f32 = jnp.bfloat16, jnp.float32
    width = place[2].astype(f32)
    report = mine[...] + swapped[...]
    hidden_along, gain_along = report[:SEQS], report[SEQS : 2 * SEQS]
    square_sum, product_sum = report[2 * SEQS :, 0:1], report[2 * SEQS :, 1:2]
    pooling = pooling_of(segments[...])
    lengths = lengths_of(segments[...])
    inverse_rms = lax.rsqrt(square_sum / width + norm_eps)
    rewards = product_sum * inverse_rms
    diagonal = iota((SEQS, SEQS), 0) == iota((SEQS, SEQS), 1)
    rewards_row = jnp.sum(jnp.where(diagonal, rewards, 0.0), axis=0, keepdims=True)
    rewards_out[...] = rewards_row
    signs = pairs[...]
    margin = jnp.sum(signs * rewards_row, axis=1, keepdims=True)
    pair_slope = loss_scale / (1.0 + jnp.exp(margin))
    grad_row = -jnp.sum(signs * pair_slope, axis=0, keepdims=True)
    reward_grad = jnp.sum(jnp.where(diagonal, grad_row, 0.0), axis=1, keepdims=True)
    gain_factor = inverse_rms * reward_grad / lengths
    hidden_factor = inverse_rms * inverse_rms * inverse_rms * (
        reward_grad * product_sum / width
    ) / lengths
    factors[0] = jnp.broadcast_to(gain_factor, (SEQS, HD))
    factors[1] = jnp.broadcast_to(hidden_factor, (SEQS, HD))
    mean_grad = (gain_factor * gain_along - hidden_factor * hidden_along).astype(bf16)
    out_grad = matmul_tn(pooling, mean_grad).astype(bf16)
    keys, values = kv_values[:, :HD], kv_values[:, HD:]
    attn = attention[...]
    prob_grad = matmul_nt(out_grad, values)
    score_grad = attn * (prob_grad - jnp.sum(attn * prob_grad, axis=1, keepdims=True))
    ratio = capped[...] / softcap_limit
    raw_grad = (score_grad * (1.0 - ratio * ratio) * (1.0 / math.sqrt(HD))).astype(bf16)
    order = member_order(place, attn.shape[0])
    query_grad[...] = matmul(order, matmul(raw_grad, keys).astype(bf16)).astype(bf16)
    kv_grad[:, :HD] = matmul_tn(raw_grad, queries[...])
    kv_grad[:, HD:] = matmul_tn(attn.astype(bf16), out_grad)


def far_kernel(place, grad, weight, far):
    width = far.shape[1] // 3
    for step in (1, 2, 3):
        start = pl.multiple_of(((place[1] // 2) ^ step) * width, width)
        far[:, (step - 1) * width : step * width] = matmul_nt(
            grad[...], weight[pl.ds(start, width), :]
        ).astype(far.dtype)


def near_kernel(
    place, segments, grad, weight, kv_mine, kv_swapped, kv_weight, hidden, gain, factors, near
):
    bf16 = jnp.bfloat16
    width = near.shape[1]
    start = pl.multiple_of(place[1] // 2 * width, width)
    order = member_order(place, near.shape[0])
    kv_grad = (kv_mine[...] + kv_swapped[...]).astype(bf16)
    kv_turned = matmul(order, kv_grad).astype(bf16)
    seq_turned = matmul_nt(order, pooling_of(segments[...])).astype(bf16)
    gain_block = gain[:, pl.ds(start, width)]
    high, low = split_high_low(
        factors[0][:, 0:1] * gain_block - factors[1][:, 0:1] * hidden[:, pl.ds(start, width)]
    )
    near[...] = (
        matmul_nt(grad[...], weight[pl.ds(start, width), :])
        + matmul_nt(kv_turned, kv_weight[...])
        + matmul(seq_turned, high)
        + matmul(seq_turned, low)
    ).astype(bf16)


def member_sum_kernel(place, own, first, second, third, out):
    f32 = jnp.float32
    rows = out.shape[0]
    out[...] = (
        (own[:rows, :].astype(f32) + first[...].astype(f32))
        + (second[...].astype(f32) + third[...].astype(f32))
    ).astype(out.dtype)


def fast_device(
    trunk_out, segment_ids, pair_order, w_query, w_key_value, w_out, norm_gain, reward_weight
):
    bf16, f32 = jnp.bfloat16, jnp.float32
    member = lax.axis_index("member")
    shard = lax.axis_index("shard")
    core = shard % 2
    col = member % 2
    local_width = trunk_out.shape[1]
    tokens = segment_ids.shape[0]
    half_width = w_query.shape[2]
    block_width = w_key_value.shape[2]
    member_rows = tokens // 4
    query_piece = w_query[0, 0]
    kv_piece = w_key_value[0, 0]
    place = jnp.stack([member, shard, jnp.int32(2 * half_width)])

    stack = [trunk_out] + [send(trunk_out, lambda m, z, k, d=d: (m, z ^ d, k)) for d in (1, 2, 3)]

    cuts = [
        lax.dynamic_slice_in_dim(query_piece, (col ^ r) * local_width, local_width, 0)
        for r in (0, 1)
    ]
    weights = [
        send(cuts[r], lambda m, z, k, r=r: (2 * k + ((m % 2) ^ r), z, m // 2))
        for r in (0, 1)
    ]

    segments, gain, kv_weight = prepare(
        place, segment_ids[None, :], norm_gain, reward_weight, kv_piece
    )
    column_own = stack_rows(place, stack)
    column_other = core_swap(column_own)
    block_shape = ((tokens, block_width), bf16)
    (kv_sent,) = local_call(kv_columns_kernel, [block_shape], place, column_own, column_other)
    kv_got = [
        send(
            kv_sent,
            lambda m, z, k, r=r: (2 * k + ((m % 2) ^ r), z, m // 2) if m % 2 == z // 2 else None,
        )
        for r in (0, 1)
    ]
    head_shape = ((tokens, HD), f32)
    query_parts = local_call(
        query_kernel, [head_shape] * 2, place, column_own, column_other, *weights
    )
    query_got = [
        send(part, lambda m, z, k, r=r: (2 * k + ((m % 2) ^ r), z, m // 2))
        for r, part in enumerate(query_parts)
    ]
    kv_part, pooled = local_call(
        kv_kernel,
        [((tokens, 2 * HD), f32), ((SEQS, block_width), f32)],
        place,
        segments,
        *kv_got,
        kv_weight,
    )
    mixed = jnp.concatenate([query_got[0] + query_got[1], kv_part], axis=1)
    swapped = core_swap(mixed)
    kv_mine, kv_swapped = height_total(mixed[:, HD:] + swapped[:, HD:], core, jnp.float16)

    out_rows, _ = lax.optimization_barrier((w_out[0], mixed))
    out_own = lax.dynamic_slice_in_dim(out_rows, core * half_width, half_width, 1)
    out_other = core_swap(
        lax.dynamic_slice_in_dim(out_rows, (1 - core) * half_width, half_width, 1)
    )

    queries, kv_values, attention, capped, message = local_call(
        forward_kernel,
        [
            ((tokens, HD), bf16),
            ((tokens, 2 * HD), bf16),
            ((tokens, tokens), f32),
            ((tokens, tokens), f32),
            ((SEQS, half_width + HD), bf16),
        ],
        place, segments, mixed, swapped, kv_mine, kv_swapped, pooled, out_own, out_other, gain,
    )
    others = [send(message, lambda m, z, k, d=d: (m, z ^ d, k)) for d in (1, 2, 3)]
    hidden, report = local_call(
        stats_kernel,
        [((SEQS, half_width), f32), ((3 * SEQS, HD), f32)],
        place, message, *others, out_own, out_other, gain,
    )
    seq_ids = jnp.arange(SEQS)[None, :]
    pairs = (pair_order[0::2][:, None] == seq_ids).astype(f32) - (
        pair_order[1::2][:, None] == seq_ids
    ).astype(f32)
    pairs = jnp.concatenate([pairs, jnp.zeros_like(pairs)], axis=0)
    query_grad, kv_grad, rewards, factors = local_call(
        backward_kernel,
        [
            ((tokens, HD), bf16),
            ((tokens, 2 * HD), f32),
            ((1, SEQS), f32),
            ((2, SEQS, HD), f32),
        ],
        place, pairs, segments, report, core_swap(report), queries, kv_values, attention, capped,
    )

    kv_mine, kv_swapped = height_total(kv_grad, core, bf16)
    (far_grad,) = local_call(
        far_kernel, [((tokens, 3 * block_width), bf16)], place, query_grad, query_piece
    )
    far_got = [
        send(far_grad[d * member_rows : (d + 1) * member_rows], lambda m, z, k, d=d: (m ^ d, z, k))
        for d in (1, 2, 3)
    ]
    (near_grad,) = local_call(
        near_kernel,
        [block_shape],
        place, segments, query_grad, query_piece, kv_mine, kv_swapped, kv_weight, hidden, gain,
        factors,
    )
    near_got = [
        send(near_grad[d * member_rows : (d + 1) * member_rows], lambda m, z, k, d=d: (m ^ d, z, k))
        for d in (1, 2, 3)
    ]
    (far_sum,) = local_call(
        member_sum_kernel, [((member_rows, 3 * block_width), bf16)], place, far_grad, *far_got
    )
    (near_sum,) = local_call(
        member_sum_kernel, [((member_rows, block_width), bf16)], place, near_grad, *near_got
    )
    pieces = [near_sum] + [far_sum[:, e * block_width : (e + 1) * block_width] for e in range(3)]
    total = 0.0
    for d in (1, 2, 3, 0):
        got = send(pieces[d], lambda m, z, k, d=d: (m, (4 * k + (z ^ d)) // 2, z % 2 ^ d % 2))
        total = total + got.astype(f32)
    return (total, rewards)


def solution(mesh):
    fast = dict(mesh.shape) == {"member": 4, "shard": 8}
    placed = (
        P("shard", "member"),
        P(),
        P(),
        P("member", "shard", None, None),
        P("member", "shard", None, None),
        P("member", "shard", None),
        P("member", None),
        P("member", None),
    )
    return jax.shard_map(
        fast_device if fast else general_device,
        mesh=mesh,
        in_specs=placed,
        out_specs=(P("member", "shard"), P("member", None)),
        check_vma=False,
    )
```

```python
import functools
import math

import jax
import jax.numpy as jnp
from jax import lax
from jax.experimental import pallas as pl
from jax.experimental.pallas import tpu as pltpu
from jax.sharding import PartitionSpec as P


HD = 128
SEQS = 8


KERNEL_VMEM = 8 << 20
softcap_limit = 20.0
loss_scale = 256.0
norm_eps = 1e-05


def from_partner(block, axis, stride):
    count = lax.axis_size(axis)
    route = []
    for low in range(count):
        high = low | 1 << stride
        if high != low and high < count:
            route += [(low, high), (high, low)]
    return lax.ppermute(block, axis, route)


def partner_swap(values, bit_number):
    return from_partner(values, "shard", bit_number)


def group_total(values, bit_list):
    for bit_number in bit_list:
        values = values + partner_swap(values, bit_number)
    return values


def pair_join(own_part, other_part, pair_side, join_axis):
    first_part = jnp.where(pair_side == 0, own_part, other_part)
    second_part = jnp.where(pair_side == 0, other_part, own_part)
    return jnp.concatenate([first_part, second_part], axis=join_axis)


def general_device(
    trunk_out, segment_ids, pair_order, w_query, w_key_value, w_out, norm_gain, reward_weight
):
    n_shard = lax.axis_size("shard")
    query_heads = n_shard // 2
    kv_count = max(1, query_heads // 8)
    group_size = query_heads // kv_count
    shard_index = lax.axis_index("shard")
    pair_side = shard_index % 2
    head_index = shard_index // 2
    block_index = shard_index % (2 * group_size) // 2
    local_rows, _ = trunk_out.shape
    features = lax.all_gather(trunk_out, "member", axis=1, tiled=True)
    gathered = lax.all_gather(features, "shard", axis=0, tiled=True)
    tok_count, model_width = gathered.shape
    half_width = model_width // 2
    half_rows = tok_count // 2
    half_head = HD // 2
    row_block = half_width // group_size
    scale_factor = 1.0 / math.sqrt(HD)
    group_bits = list(range((2 * group_size).bit_length() - 1))
    query_piece = w_query[0, 0]
    kv_piece = w_key_value[0, 0]
    out_rows = w_out[0]
    gain_vector = norm_gain[0]
    head_weight = reward_weight[0]
    positions = jnp.arange(tok_count)
    own_start = pair_side * half_rows
    own_positions = own_start + jnp.arange(half_rows)
    own_segments = lax.dynamic_slice_in_dim(segment_ids, own_start, half_rows, 0)
    allowed = (own_segments[:, None] == segment_ids[None, :]) & (
        positions[None, :] <= own_positions[:, None]
    )
    member_of = jnp.arange(SEQS)[:, None] == segment_ids[None, :]
    pooling = member_of.astype(jnp.bfloat16)
    lengths = jnp.sum(member_of.astype(jnp.float32), axis=1)
    own_pooling = lax.dynamic_slice_in_dim(pooling, own_start, half_rows, 1)
    half_features = lax.dynamic_slice_in_dim(gathered, pair_side * half_width, half_width, 1)
    query_partial = jnp.dot(half_features, query_piece, preferred_element_type=jnp.float32)
    kept_rows = lax.dynamic_slice_in_dim(query_partial, own_start, half_rows, 0)
    sent_rows = lax.dynamic_slice_in_dim(query_partial, half_rows - own_start, half_rows, 0)
    queries = (kept_rows + partner_swap(sent_rows, 0)).astype(jnp.bfloat16)
    kv_features = lax.dynamic_slice_in_dim(half_features, block_index * row_block, row_block, 1)
    kv_values = group_total(
        jnp.dot(kv_features, kv_piece, preferred_element_type=jnp.float32), group_bits
    ).astype(jnp.bfloat16)
    key_full = kv_values[:, :HD]
    value_full = kv_values[:, HD:]
    raw_scores = (
        jnp.einsum("td,sd->ts", queries, key_full, preferred_element_type=jnp.float32)
        * scale_factor
    )
    capped = softcap_limit * jnp.tanh(raw_scores / softcap_limit)
    weights_exp = jnp.where(allowed, jnp.exp(capped), 0.0)
    attention = weights_exp / jnp.sum(weights_exp, axis=1, keepdims=True)
    attention_low = attention.astype(jnp.bfloat16)
    attended = jnp.dot(attention_low, value_full, preferred_element_type=jnp.float32).astype(
        jnp.bfloat16
    )
    seq_part = jnp.dot(own_pooling, attended, preferred_element_type=jnp.float32)
    seq_total = seq_part + partner_swap(seq_part, 0)
    seq_mean = (seq_total / lengths[:, None]).astype(jnp.bfloat16)
    own_dims = lax.dynamic_slice_in_dim(seq_mean, pair_side * half_head, half_head, 1)
    head_part = jnp.dot(own_dims, out_rows, preferred_element_type=jnp.float32)
    pooled_attn = lax.psum(head_part, "shard")
    pooled_input = jnp.dot(pooling, gathered, preferred_element_type=jnp.float32) / lengths[:, None]
    hidden = pooled_input + pooled_attn
    inverse_rms = lax.rsqrt(jnp.mean(hidden * hidden, axis=1) + norm_eps)
    normed = hidden * inverse_rms[:, None] * gain_vector
    rewards = jnp.sum(normed * head_weight, axis=1)
    seq_ids = jnp.arange(SEQS)
    chosen = (pair_order[0::2][:, None] == seq_ids[None, :]).astype(jnp.float32)
    rejected = (pair_order[1::2][:, None] == seq_ids[None, :]).astype(jnp.float32)
    margin = jnp.sum(chosen * rewards, axis=1) - jnp.sum(rejected * rewards, axis=1)
    pair_slope = loss_scale * jax.nn.sigmoid(-margin)
    reward_grad = jnp.sum(rejected * pair_slope[:, None], axis=0) - jnp.sum(
        chosen * pair_slope[:, None], axis=0
    )
    scaled_grad = reward_grad[:, None] * head_weight * gain_vector
    hidden_grad = inverse_rms[:, None] * (
        scaled_grad
        - hidden * (inverse_rms**2)[:, None] * jnp.mean(hidden * scaled_grad, axis=1, keepdims=True)
    )
    per_token = hidden_grad / lengths[:, None]
    grad_low = hidden_grad.astype(jnp.bfloat16)
    grad_dims = (
        jnp.einsum("jd,ed->je", grad_low, out_rows, preferred_element_type=jnp.float32)
        / lengths[:, None]
    )
    mean_grad = pair_join(grad_dims, partner_swap(grad_dims, 0), pair_side, 1)
    out_grad = jnp.take(mean_grad, own_segments, axis=0).astype(jnp.bfloat16)
    prob_grad = jnp.einsum("td,sd->ts", out_grad, value_full, preferred_element_type=jnp.float32)
    score_grad = attention * (prob_grad - jnp.sum(attention * prob_grad, axis=1, keepdims=True))
    raw_grad = (score_grad * (1.0 - (capped / softcap_limit) ** 2) * scale_factor).astype(
        jnp.bfloat16
    )
    query_grad = jnp.dot(raw_grad, key_full, preferred_element_type=jnp.float32).astype(
        jnp.bfloat16
    )
    key_grad = jnp.einsum("ts,td->sd", raw_grad, queries, preferred_element_type=jnp.float32)
    value_grad = jnp.einsum(
        "ts,td->sd", attention_low, out_grad, preferred_element_type=jnp.float32
    )
    kv_grad = group_total(jnp.concatenate([key_grad, value_grad], axis=1), group_bits).astype(
        jnp.bfloat16
    )
    query_wire = lax.optimization_barrier(query_grad).astype(jnp.float32)
    query_all = pair_join(
        query_grad, partner_swap(query_wire, 0).astype(jnp.bfloat16), pair_side, 0
    )
    grad_half = jnp.einsum("td,rd->tr", query_all, query_piece, preferred_element_type=jnp.float32)
    kv_term = jnp.einsum("te,re->tr", kv_grad, kv_piece, preferred_element_type=jnp.float32)
    start_col = block_index * row_block
    grad_half = lax.dynamic_update_slice_in_dim(
        grad_half,
        lax.dynamic_slice_in_dim(grad_half, start_col, row_block, 1) + kv_term,
        start_col,
        1,
    )
    pair_rows = 2 * local_rows
    start_row = head_index * pair_rows
    pair_segments = lax.dynamic_slice_in_dim(segment_ids, start_row, pair_rows, 0)
    token_half = lax.dynamic_slice_in_dim(per_token, pair_side * half_width, half_width, 1)
    direct = jnp.take(token_half, pair_segments, axis=0)
    grad_half = lax.dynamic_update_slice_in_dim(
        grad_half,
        lax.dynamic_slice_in_dim(grad_half, start_row, pair_rows, 0) + direct,
        start_row,
        0,
    )
    by_member = lax.psum_scatter(grad_half, "member", scatter_dimension=0, tiled=True)
    member_rows = by_member.shape[0]
    placed = lax.dynamic_update_slice_in_dim(
        jnp.zeros((member_rows, model_width), jnp.float32), by_member, pair_side * half_width, 1
    )
    trunk_grad = lax.psum_scatter(placed, "shard", scatter_dimension=1, tiled=True)
    return (trunk_grad, rewards[None])


def route_pairs(target):
    pairs = []
    for member in range(4):
        for height in range(4):
            for core in range(2):
                to = target(member, height, core)
                if to is not None:
                    pairs.append((member * 8 + height * 2 + core, to[0] * 8 + to[1] * 2 + to[2]))
    return pairs


def send(block, target):
    return lax.ppermute(block, ("member", "shard"), route_pairs(target))


def core_swap(block):
    return send(block, lambda m, z, k: (m, z, 1 - k))


def matmul(left, right):
    return jnp.dot(left, right, preferred_element_type=jnp.float32)


def matmul_nt(left, right):
    return lax.dot_general(
        left, right, (((1,), (1,)), ((), ())), preferred_element_type=jnp.float32
    )


def matmul_tn(left, right):
    return lax.dot_general(
        left, right, (((0,), (0,)), ((), ())), preferred_element_type=jnp.float32
    )


def height_total(block, core, wire):
    sent = block.astype(wire)
    near = send(sent, lambda m, z, k: (m, z ^ (1 + k), k))
    half = jnp.where(core == 0, sent[:, :HD], sent[:, HD:])
    far = send(half, lambda m, z, k: (m, z ^ 3, k)).astype(jnp.float32)
    zero = jnp.zeros_like(far)
    spread = jnp.concatenate(
        [jnp.where(core == 0, far, zero), jnp.where(core == 0, zero, far)], axis=1
    )
    mine = jnp.where(core == 0, sent.astype(jnp.float32), 0.0) + near.astype(jnp.float32) + spread
    return mine, core_swap(mine)


def split_high_low(value):
    high = value.astype(jnp.bfloat16)
    return high, (value - high.astype(jnp.float32)).astype(jnp.bfloat16)


def iota(shape, dimension):
    return lax.broadcasted_iota(jnp.int32, shape, dimension)


def one_hot(condition):
    return condition.astype(jnp.float32).astype(jnp.bfloat16)


def pooling_of(segments):
    return one_hot(iota((SEQS, segments.shape[1]), 0) == segments)


def lengths_of(segments):
    return jnp.sum(
        (iota((SEQS, segments.shape[1]), 0) == segments).astype(jnp.float32), axis=1, keepdims=True
    )


def here():
    return lax.axis_index("member"), lax.axis_index("shard")


def local_call(kernel, outputs, *operands):
    vmem = pl.BlockSpec(memory_space=pltpu.VMEM)
    return pl.pallas_call(
        kernel,
        out_shape=[jax.ShapeDtypeStruct(shape, dtype) for shape, dtype in outputs],
        in_specs=[vmem] * len(operands),
        out_specs=[vmem] * len(outputs),
        compiler_params=pltpu.CompilerParams(vmem_limit_bytes=KERNEL_VMEM),
    )(*operands)


def prepare_kernel(
    segment_ids, norm_gain, reward_weight, weight, trunk,
    segments_out, gain_out, weight_out, trunk_out, head_weight, sems,
):
    place = here()
    width = gain_out.shape[1]
    start = pl.multiple_of(place[1] % 2 * width, width)
    copies = [
        pltpu.make_async_copy(weight, weight_out, sems.at[0]),
        pltpu.make_async_copy(segment_ids, segments_out, sems.at[1]),
        pltpu.make_async_copy(norm_gain.at[:, pl.ds(start, width)], gain_out, sems.at[2]),
        pltpu.make_async_copy(reward_weight.at[:, pl.ds(start, width)], head_weight, sems.at[3]),
        pltpu.make_async_copy(trunk, trunk_out, sems.at[4]),
    ]
    for copy in copies:
        copy.start()
    for copy in copies:
        copy.wait()
    gain_out[...] = gain_out[...] * head_weight[...]


def prepare(segments, norm_gain, reward_weight, weight, trunk):
    width = norm_gain.shape[1] // 2
    return pl.pallas_call(
        prepare_kernel,
        out_shape=[
            jax.ShapeDtypeStruct(segments.shape, segments.dtype),
            jax.ShapeDtypeStruct((1, width), norm_gain.dtype),
            jax.ShapeDtypeStruct(weight.shape, weight.dtype),
            jax.ShapeDtypeStruct(trunk.shape, trunk.dtype),
        ],
        in_specs=[pl.BlockSpec(memory_space=pl.ANY)] * 5,
        out_specs=[pl.BlockSpec(memory_space=pltpu.VMEM)] * 4,
        scratch_shapes=[
            pltpu.VMEM((1, width), reward_weight.dtype),
            pltpu.SemaphoreType.DMA((5,)),
        ],
        compiler_params=pltpu.CompilerParams(vmem_limit_bytes=KERNEL_VMEM),
    )(segments, norm_gain, reward_weight, weight, trunk)


def stack_kernel(*refs):
    place = here()
    pieces, out, sems = refs[:-2], refs[-2], refs[-1]
    rows = pieces[0].shape[0]
    copies = []
    for step, ref in enumerate(pieces):
        start = pl.multiple_of(((place[1] // 2) ^ step) * rows, rows)
        copies.append(pltpu.make_async_copy(ref, out.at[pl.ds(start, rows), :], sems.at[step]))
    for copy in copies:
        copy.start()
    for copy in copies:
        copy.wait()


def stack_rows(blocks):
    rows, width = blocks[0].shape
    return pl.pallas_call(
        stack_kernel,
        out_shape=jax.ShapeDtypeStruct((len(blocks) * rows, width), blocks[0].dtype),
        in_specs=[pl.BlockSpec(memory_space=pl.ANY)] * len(blocks),
        out_specs=pl.BlockSpec(memory_space=pltpu.VMEM),
        scratch_shapes=[pltpu.SemaphoreType.DMA((len(blocks),))],
        compiler_params=pltpu.CompilerParams(vmem_limit_bytes=KERNEL_VMEM),
    )(*blocks)


def kv_columns_kernel(own, other, out):
    place = here()
    width = out.shape[1]
    rows = own.shape[0] // 4
    core = place[1] % 2
    start = pl.multiple_of(place[1] // 2 % 2 * width, width)
    for source, side in ((own, core), (other, 1 - core)):
        for step in range(4):
            to = pl.multiple_of((2 * step + side) * rows, rows)
            out[pl.ds(to, rows), :] = source[step * rows : (step + 1) * rows, pl.ds(start, width)]


def query_kernel(own, other, weight, out):
    place = here()
    rows = own.shape[0] // 4
    core = place[1] % 2
    for source, side in ((own, core), (other, 1 - core)):
        part = matmul(source[...], weight[...])
        for step in range(4):
            to = pl.multiple_of((2 * step + side) * rows, rows)
            out[pl.ds(to, rows), :] = part[step * rows : (step + 1) * rows]


def kv_kernel(segments, first, second, weight, out, pooled):
    place = here()
    far = (place[1] // 4) ^ (place[0] % 2)
    columns = jnp.where(far == 0, first[...], second[...])
    out[...] = matmul(columns, weight[...])
    pooled[...] = matmul(pooling_of(segments[...]), columns) / lengths_of(segments[...])


def forward_kernel(
    segments, mine, swapped, kv_mine, kv_swapped, pooled, out_own, out_other, gain,
    queries_out, kv_out, attention_out, capped_out, message,
):
    bf16 = jnp.bfloat16
    place = here()
    core, height = place[1] % 2, place[1] // 2
    queries = (mine[:, :HD] + swapped[:, :HD]).astype(bf16)
    kv_values = (kv_mine[...] + kv_swapped[...]).astype(bf16)
    queries_out[...] = queries
    kv_out[...] = kv_values
    keys, values = kv_values[:, :HD], kv_values[:, HD:]
    pooling = pooling_of(segments[...])
    lengths = lengths_of(segments[...])
    tokens = pooling.shape[1]
    same = matmul_tn(pooling, pooling) > 0.5
    allowed = same & (iota((tokens, tokens), 1) <= iota((tokens, tokens), 0))
    raw_scores = matmul_nt(queries, keys) * (1.0 / math.sqrt(HD))
    capped = softcap_limit * jnp.tanh(raw_scores / softcap_limit)
    weights_exp = jnp.where(allowed, jnp.exp(capped), 0.0)
    attention = weights_exp / jnp.sum(weights_exp, axis=1, keepdims=True)
    attention_out[...] = attention
    capped_out[...] = capped
    attended = matmul(attention.astype(bf16), values).astype(bf16)
    seq_mean = (matmul(pooling, attended) / lengths).astype(bf16)
    half = out_own.shape[0]
    low, high = seq_mean[:, :half], seq_mean[:, half:]
    part = matmul(jnp.where(core == 0, low, high), out_own[...]) + matmul(
        jnp.where(core == 0, high, low), out_other[...]
    )
    width = pooled.shape[1]
    part = jnp.concatenate(
        [
            part[:, n * width : (n + 1) * width] + jnp.where(height == n, pooled[...], 0.0)
            for n in range(part.shape[1] // width)
        ],
        axis=1,
    )
    product_high, product_low = split_high_low(jnp.sum(part * gain[...], axis=1, keepdims=True))
    lane = iota((SEQS, HD), 1)
    message[:, : part.shape[1]] = part.astype(bf16)
    message[:, part.shape[1] :] = jnp.where(
        lane == 0,
        product_high.astype(jnp.float32),
        jnp.where(lane == 1, product_low.astype(jnp.float32), 0.0),
    ).astype(bf16)


def stats_kernel(
    first, second, third, fourth, out_own, out_other, gain, hidden_out, report
):
    core = here()[1] % 2
    half_width = hidden_out.shape[1]
    f32 = jnp.float32
    total = (first[...].astype(f32) + second[...].astype(f32)) + (
        third[...].astype(f32) + fourth[...].astype(f32)
    )
    hidden = total[:, :half_width]
    hidden_out[...] = hidden
    stacked = jnp.concatenate([hidden, jnp.broadcast_to(gain[...], hidden.shape)], axis=0)
    stacked = stacked.astype(jnp.bfloat16)
    along_own = matmul_nt(stacked, out_own[...])
    along_other = matmul_nt(stacked, out_other[...])
    half = along_own.shape[1]
    report[: 2 * SEQS, :half] = jnp.where(core == 0, along_own, along_other)
    report[: 2 * SEQS, half:] = jnp.where(core == 0, along_other, along_own)
    squares = jnp.sum(hidden * hidden, axis=1, keepdims=True)
    products = total[:, half_width : half_width + 1] + total[:, half_width + 1 : half_width + 2]
    lane = iota((SEQS, HD), 1)
    report[2 * SEQS :, :] = jnp.where(lane == 0, squares, jnp.where(lane == 1, products, 0.0))


def member_order(place, tokens):
    rows = tokens // 4
    position = iota((tokens, tokens), 0)
    token = rows * (place[0] ^ (position // rows)) + position % rows
    return one_hot(iota((tokens, tokens), 1) == token)


def backward_kernel(
    pairs, segments, mine, swapped, queries, kv_values, attention, capped,
    query_grad, kv_grad, rewards_out, factors, *, full_width,
):
    bf16 = jnp.bfloat16
    width = full_width
    report = mine[...] + swapped[...]
    hidden_along, gain_along = report[:SEQS], report[SEQS : 2 * SEQS]
    square_sum, product_sum = report[2 * SEQS :, 0:1], report[2 * SEQS :, 1:2]
    pooling = pooling_of(segments[...])
    lengths = lengths_of(segments[...])
    inverse_rms = lax.rsqrt(square_sum / width + norm_eps)
    rewards = product_sum * inverse_rms
    diagonal = iota((SEQS, SEQS), 0) == iota((SEQS, SEQS), 1)
    rewards_row = jnp.sum(jnp.where(diagonal, rewards, 0.0), axis=0, keepdims=True)
    rewards_out[...] = rewards_row
    signs = pairs[...]
    margin = jnp.sum(signs * rewards_row, axis=1, keepdims=True)
    pair_slope = loss_scale / (1.0 + jnp.exp(margin))
    grad_row = -jnp.sum(signs * pair_slope, axis=0, keepdims=True)
    reward_grad = jnp.sum(jnp.where(diagonal, grad_row, 0.0), axis=1, keepdims=True)
    gain_factor = inverse_rms * reward_grad / lengths
    hidden_factor = inverse_rms * inverse_rms * inverse_rms * (
        reward_grad * product_sum / width
    ) / lengths
    factors[0] = jnp.broadcast_to(gain_factor, (SEQS, HD))
    factors[1] = jnp.broadcast_to(hidden_factor, (SEQS, HD))
    mean_grad = (gain_factor * gain_along - hidden_factor * hidden_along).astype(bf16)
    out_grad = matmul_tn(pooling, mean_grad).astype(bf16)
    keys, values = kv_values[:, :HD], kv_values[:, HD:]
    attn = attention[...]
    prob_grad = matmul_nt(out_grad, values)
    score_grad = attn * (prob_grad - jnp.sum(attn * prob_grad, axis=1, keepdims=True))
    ratio = capped[...] / softcap_limit
    raw_grad = (score_grad * (1.0 - ratio * ratio) * (1.0 / math.sqrt(HD))).astype(bf16)
    order = member_order(here(), attn.shape[0])
    query_grad[...] = matmul(order, matmul(raw_grad, keys).astype(bf16)).astype(bf16)
    kv_grad[:, :HD] = matmul_tn(raw_grad, queries[...])
    kv_grad[:, HD:] = matmul_tn(attn.astype(bf16), out_grad)


def far_kernel(grad, weight, far):
    place = here()
    width = far.shape[1] // 3
    for step in (1, 2, 3):
        start = pl.multiple_of(((place[1] // 2) ^ step) * width, width)
        far[:, (step - 1) * width : step * width] = matmul_nt(
            grad[...], weight[pl.ds(start, width), :]
        ).astype(far.dtype)


def near_kernel(
    segments, grad, weight, kv_mine, kv_swapped, kv_weight, hidden, gain, factors, near
):
    bf16 = jnp.bfloat16
    place = here()
    width = near.shape[1]
    start = pl.multiple_of(place[1] // 2 * width, width)
    order = member_order(place, near.shape[0])
    kv_grad = (kv_mine[...] + kv_swapped[...]).astype(bf16)
    kv_turned = matmul(order, kv_grad).astype(bf16)
    seq_turned = matmul_nt(order, pooling_of(segments[...])).astype(bf16)
    gain_block = gain[:, pl.ds(start, width)]
    high, low = split_high_low(
        factors[0][:, 0:1] * gain_block - factors[1][:, 0:1] * hidden[:, pl.ds(start, width)]
    )
    near[...] = (
        matmul_nt(grad[...], weight[pl.ds(start, width), :])
        + matmul_nt(kv_turned, kv_weight[...])
        + matmul(seq_turned, high)
        + matmul(seq_turned, low)
    ).astype(bf16)


def member_sum_kernel(own, first, second, third, out):
    f32 = jnp.float32
    rows = out.shape[0]
    out[...] = (
        (own[:rows, :].astype(f32) + first[...].astype(f32))
        + (second[...].astype(f32) + third[...].astype(f32))
    ).astype(out.dtype)


def fast_device(
    trunk_out, segment_ids, pair_order, w_query, w_key_value, w_out, norm_gain, reward_weight
):
    bf16, f32 = jnp.bfloat16, jnp.float32
    member = lax.axis_index("member")
    shard = lax.axis_index("shard")
    core = shard % 2
    col = member % 2
    local_width = trunk_out.shape[1]
    tokens = segment_ids.shape[0]
    half_width = w_query.shape[2]
    block_width = w_key_value.shape[2]
    member_rows = tokens // 4
    query_piece = w_query[0, 0]
    kv_piece = w_key_value[0, 0]

    stack = [send(trunk_out, lambda m, z, k, d=d: (m, z ^ d, k)) for d in (1, 2, 3)]

    cuts = [
        lax.dynamic_slice_in_dim(query_piece, (col ^ r) * local_width, local_width, 0)
        for r in (0, 1)
    ]
    weights = [
        send(cuts[r], lambda m, z, k, r=r: (2 * k + ((m % 2) ^ r), z, m // 2))
        for r in (0, 1)
    ]

    segments, gain, kv_weight, trunk_near = prepare(
        segment_ids[None, :], norm_gain, reward_weight, kv_piece, trunk_out
    )
    column_own = stack_rows([trunk_near] + stack)
    column_other = core_swap(column_own)
    block_shape = ((tokens, block_width), bf16)
    (kv_sent,) = local_call(kv_columns_kernel, [block_shape], column_own, column_other)
    kv_got = [
        send(
            kv_sent,
            lambda m, z, k, r=r: (2 * k + ((m % 2) ^ r), z, m // 2) if m % 2 == z // 2 else None,
        )
        for r in (0, 1)
    ]
    head_shape = ((tokens, HD), f32)
    query_parts = [
        local_call(query_kernel, [head_shape], column_own, column_other, weights[r])[0]
        for r in (0, 1)
    ]
    query_got = [
        send(part, lambda m, z, k, r=r: (2 * k + ((m % 2) ^ r), z, m // 2))
        for r, part in enumerate(query_parts)
    ]
    kv_part, pooled = local_call(
        kv_kernel,
        [((tokens, 2 * HD), f32), ((SEQS, block_width), f32)],
        segments,
        *kv_got,
        kv_weight,
    )
    mixed = jnp.concatenate([query_got[0] + query_got[1], kv_part], axis=1)
    swapped = core_swap(mixed)
    kv_mine, kv_swapped = height_total(mixed[:, HD:] + swapped[:, HD:], core, jnp.float16)

    out_rows, _ = lax.optimization_barrier((w_out[0], mixed))
    out_own = lax.dynamic_slice_in_dim(out_rows, core * half_width, half_width, 1)
    out_other = core_swap(
        lax.dynamic_slice_in_dim(out_rows, (1 - core) * half_width, half_width, 1)
    )

    queries, kv_values, attention, capped, message = local_call(
        forward_kernel,
        [
            ((tokens, HD), bf16),
            ((tokens, 2 * HD), bf16),
            ((tokens, tokens), f32),
            ((tokens, tokens), f32),
            ((SEQS, half_width + HD), bf16),
        ],
        segments, mixed, swapped, kv_mine, kv_swapped, pooled, out_own, out_other, gain,
    )
    others = [send(message, lambda m, z, k, d=d: (m, z ^ d, k)) for d in (1, 2, 3)]
    hidden, report = local_call(
        stats_kernel,
        [((SEQS, half_width), f32), ((3 * SEQS, HD), f32)],
        message, *others, out_own, out_other, gain,
    )
    seq_ids = jnp.arange(SEQS)[None, :]
    pairs = (pair_order[0::2][:, None] == seq_ids).astype(f32) - (
        pair_order[1::2][:, None] == seq_ids
    ).astype(f32)
    pairs = jnp.concatenate([pairs, jnp.zeros_like(pairs)], axis=0)
    query_grad, kv_grad, rewards, factors = local_call(
        functools.partial(backward_kernel, full_width=float(2 * half_width)),
        [
            ((tokens, HD), bf16),
            ((tokens, 2 * HD), f32),
            ((1, SEQS), f32),
            ((2, SEQS, HD), f32),
        ],
        pairs, segments, report, core_swap(report), queries, kv_values, attention, capped,
    )

    kv_mine, kv_swapped = height_total(kv_grad, core, bf16)
    (far_grad,) = local_call(
        far_kernel, [((tokens, 3 * block_width), bf16)], query_grad, query_piece
    )
    far_got = [
        send(far_grad[d * member_rows : (d + 1) * member_rows], lambda m, z, k, d=d: (m ^ d, z, k))
        for d in (1, 2, 3)
    ]
    (near_grad,) = local_call(
        near_kernel,
        [block_shape],
        segments, query_grad, query_piece, kv_mine, kv_swapped, kv_weight, hidden, gain,
        factors,
    )
    near_got = [
        send(near_grad[d * member_rows : (d + 1) * member_rows], lambda m, z, k, d=d: (m ^ d, z, k))
        for d in (1, 2, 3)
    ]
    (far_sum,) = local_call(
        member_sum_kernel, [((member_rows, 3 * block_width), bf16)], far_grad, *far_got
    )
    (near_sum,) = local_call(
        member_sum_kernel, [((member_rows, block_width), bf16)], near_grad, *near_got
    )
    pieces = [near_sum] + [far_sum[:, e * block_width : (e + 1) * block_width] for e in range(3)]
    total = 0.0
    for d in (1, 2, 3, 0):
        got = send(pieces[d], lambda m, z, k, d=d: (m, (4 * k + (z ^ d)) // 2, z % 2 ^ d % 2))
        total = total + got.astype(f32)
    return (total, rewards)


def solution(mesh):
    fast = dict(mesh.shape) == {"member": 4, "shard": 8}
    placed = (
        P("shard", "member"),
        P(),
        P(),
        P("member", "shard", None, None),
        P("member", "shard", None, None),
        P("member", "shard", None),
        P("member", None),
        P("member", None),
    )
    return jax.shard_map(
        fast_device if fast else general_device,
        mesh=mesh,
        in_specs=placed,
        out_specs=(P("member", "shard"), P("member", None)),
        check_vma=False,
    )
```

```python
import functools
import math

import jax
import jax.numpy as jnp
from jax import lax
from jax.experimental import pallas as pl
from jax.experimental.pallas import tpu as pltpu
from jax.sharding import PartitionSpec as P


HD = 128
SEQS = 8


KERNEL_VMEM = 8 << 20
softcap_limit = 20.0
loss_scale = 256.0
norm_eps = 1e-05


def from_partner(block, axis, stride):
    count = lax.axis_size(axis)
    route = []
    for low in range(count):
        high = low | 1 << stride
        if high != low and high < count:
            route += [(low, high), (high, low)]
    return lax.ppermute(block, axis, route)


def partner_swap(values, bit_number):
    return from_partner(values, "shard", bit_number)


def group_total(values, bit_list):
    for bit_number in bit_list:
        values = values + partner_swap(values, bit_number)
    return values


def pair_join(own_part, other_part, pair_side, join_axis):
    first_part = jnp.where(pair_side == 0, own_part, other_part)
    second_part = jnp.where(pair_side == 0, other_part, own_part)
    return jnp.concatenate([first_part, second_part], axis=join_axis)


def general_device(
    trunk_out, segment_ids, pair_order, w_query, w_key_value, w_out, norm_gain, reward_weight
):
    n_shard = lax.axis_size("shard")
    query_heads = n_shard // 2
    kv_count = max(1, query_heads // 8)
    group_size = query_heads // kv_count
    shard_index = lax.axis_index("shard")
    pair_side = shard_index % 2
    head_index = shard_index // 2
    block_index = shard_index % (2 * group_size) // 2
    local_rows, _ = trunk_out.shape
    features = lax.all_gather(trunk_out, "member", axis=1, tiled=True)
    gathered = lax.all_gather(features, "shard", axis=0, tiled=True)
    tok_count, model_width = gathered.shape
    half_width = model_width // 2
    half_rows = tok_count // 2
    half_head = HD // 2
    row_block = half_width // group_size
    scale_factor = 1.0 / math.sqrt(HD)
    group_bits = list(range((2 * group_size).bit_length() - 1))
    query_piece = w_query[0, 0]
    kv_piece = w_key_value[0, 0]
    out_rows = w_out[0]
    gain_vector = norm_gain[0]
    head_weight = reward_weight[0]
    positions = jnp.arange(tok_count)
    own_start = pair_side * half_rows
    own_positions = own_start + jnp.arange(half_rows)
    own_segments = lax.dynamic_slice_in_dim(segment_ids, own_start, half_rows, 0)
    allowed = (own_segments[:, None] == segment_ids[None, :]) & (
        positions[None, :] <= own_positions[:, None]
    )
    member_of = jnp.arange(SEQS)[:, None] == segment_ids[None, :]
    pooling = member_of.astype(jnp.bfloat16)
    lengths = jnp.sum(member_of.astype(jnp.float32), axis=1)
    own_pooling = lax.dynamic_slice_in_dim(pooling, own_start, half_rows, 1)
    half_features = lax.dynamic_slice_in_dim(gathered, pair_side * half_width, half_width, 1)
    query_partial = jnp.dot(half_features, query_piece, preferred_element_type=jnp.float32)
    kept_rows = lax.dynamic_slice_in_dim(query_partial, own_start, half_rows, 0)
    sent_rows = lax.dynamic_slice_in_dim(query_partial, half_rows - own_start, half_rows, 0)
    queries = (kept_rows + partner_swap(sent_rows, 0)).astype(jnp.bfloat16)
    kv_features = lax.dynamic_slice_in_dim(half_features, block_index * row_block, row_block, 1)
    kv_values = group_total(
        jnp.dot(kv_features, kv_piece, preferred_element_type=jnp.float32), group_bits
    ).astype(jnp.bfloat16)
    key_full = kv_values[:, :HD]
    value_full = kv_values[:, HD:]
    raw_scores = (
        jnp.einsum("td,sd->ts", queries, key_full, preferred_element_type=jnp.float32)
        * scale_factor
    )
    capped = softcap_limit * jnp.tanh(raw_scores / softcap_limit)
    weights_exp = jnp.where(allowed, jnp.exp(capped), 0.0)
    attention = weights_exp / jnp.sum(weights_exp, axis=1, keepdims=True)
    attention_low = attention.astype(jnp.bfloat16)
    attended = jnp.dot(attention_low, value_full, preferred_element_type=jnp.float32).astype(
        jnp.bfloat16
    )
    seq_part = jnp.dot(own_pooling, attended, preferred_element_type=jnp.float32)
    seq_total = seq_part + partner_swap(seq_part, 0)
    seq_mean = (seq_total / lengths[:, None]).astype(jnp.bfloat16)
    own_dims = lax.dynamic_slice_in_dim(seq_mean, pair_side * half_head, half_head, 1)
    head_part = jnp.dot(own_dims, out_rows, preferred_element_type=jnp.float32)
    pooled_attn = lax.psum(head_part, "shard")
    pooled_input = jnp.dot(pooling, gathered, preferred_element_type=jnp.float32) / lengths[:, None]
    hidden = pooled_input + pooled_attn
    inverse_rms = lax.rsqrt(jnp.mean(hidden * hidden, axis=1) + norm_eps)
    normed = hidden * inverse_rms[:, None] * gain_vector
    rewards = jnp.sum(normed * head_weight, axis=1)
    seq_ids = jnp.arange(SEQS)
    chosen = (pair_order[0::2][:, None] == seq_ids[None, :]).astype(jnp.float32)
    rejected = (pair_order[1::2][:, None] == seq_ids[None, :]).astype(jnp.float32)
    margin = jnp.sum(chosen * rewards, axis=1) - jnp.sum(rejected * rewards, axis=1)
    pair_slope = loss_scale * jax.nn.sigmoid(-margin)
    reward_grad = jnp.sum(rejected * pair_slope[:, None], axis=0) - jnp.sum(
        chosen * pair_slope[:, None], axis=0
    )
    scaled_grad = reward_grad[:, None] * head_weight * gain_vector
    hidden_grad = inverse_rms[:, None] * (
        scaled_grad
        - hidden * (inverse_rms**2)[:, None] * jnp.mean(hidden * scaled_grad, axis=1, keepdims=True)
    )
    per_token = hidden_grad / lengths[:, None]
    grad_low = hidden_grad.astype(jnp.bfloat16)
    grad_dims = (
        jnp.einsum("jd,ed->je", grad_low, out_rows, preferred_element_type=jnp.float32)
        / lengths[:, None]
    )
    mean_grad = pair_join(grad_dims, partner_swap(grad_dims, 0), pair_side, 1)
    out_grad = jnp.take(mean_grad, own_segments, axis=0).astype(jnp.bfloat16)
    prob_grad = jnp.einsum("td,sd->ts", out_grad, value_full, preferred_element_type=jnp.float32)
    score_grad = attention * (prob_grad - jnp.sum(attention * prob_grad, axis=1, keepdims=True))
    raw_grad = (score_grad * (1.0 - (capped / softcap_limit) ** 2) * scale_factor).astype(
        jnp.bfloat16
    )
    query_grad = jnp.dot(raw_grad, key_full, preferred_element_type=jnp.float32).astype(
        jnp.bfloat16
    )
    key_grad = jnp.einsum("ts,td->sd", raw_grad, queries, preferred_element_type=jnp.float32)
    value_grad = jnp.einsum(
        "ts,td->sd", attention_low, out_grad, preferred_element_type=jnp.float32
    )
    kv_grad = group_total(jnp.concatenate([key_grad, value_grad], axis=1), group_bits).astype(
        jnp.bfloat16
    )
    query_wire = lax.optimization_barrier(query_grad).astype(jnp.float32)
    query_all = pair_join(
        query_grad, partner_swap(query_wire, 0).astype(jnp.bfloat16), pair_side, 0
    )
    grad_half = jnp.einsum("td,rd->tr", query_all, query_piece, preferred_element_type=jnp.float32)
    kv_term = jnp.einsum("te,re->tr", kv_grad, kv_piece, preferred_element_type=jnp.float32)
    start_col = block_index * row_block
    grad_half = lax.dynamic_update_slice_in_dim(
        grad_half,
        lax.dynamic_slice_in_dim(grad_half, start_col, row_block, 1) + kv_term,
        start_col,
        1,
    )
    pair_rows = 2 * local_rows
    start_row = head_index * pair_rows
    pair_segments = lax.dynamic_slice_in_dim(segment_ids, start_row, pair_rows, 0)
    token_half = lax.dynamic_slice_in_dim(per_token, pair_side * half_width, half_width, 1)
    direct = jnp.take(token_half, pair_segments, axis=0)
    grad_half = lax.dynamic_update_slice_in_dim(
        grad_half,
        lax.dynamic_slice_in_dim(grad_half, start_row, pair_rows, 0) + direct,
        start_row,
        0,
    )
    by_member = lax.psum_scatter(grad_half, "member", scatter_dimension=0, tiled=True)
    member_rows = by_member.shape[0]
    placed = lax.dynamic_update_slice_in_dim(
        jnp.zeros((member_rows, model_width), jnp.float32), by_member, pair_side * half_width, 1
    )
    trunk_grad = lax.psum_scatter(placed, "shard", scatter_dimension=1, tiled=True)
    return (trunk_grad, rewards[None])


def route_pairs(target):
    pairs = []
    for member in range(4):
        for height in range(4):
            for core in range(2):
                to = target(member, height, core)
                if to is not None:
                    pairs.append((member * 8 + height * 2 + core, to[0] * 8 + to[1] * 2 + to[2]))
    return pairs


def send(block, target):
    return lax.ppermute(block, ("member", "shard"), route_pairs(target))


def core_swap(block):
    return send(block, lambda m, z, k: (m, z, 1 - k))


def matmul(left, right):
    return jnp.dot(left, right, preferred_element_type=jnp.float32)


def matmul_nt(left, right):
    return lax.dot_general(
        left, right, (((1,), (1,)), ((), ())), preferred_element_type=jnp.float32
    )


def matmul_tn(left, right):
    return lax.dot_general(
        left, right, (((0,), (0,)), ((), ())), preferred_element_type=jnp.float32
    )


def height_total(block, core, wire, beside=None):
    sent = block.astype(wire)
    near = send(sent, lambda m, z, k: (m, z ^ (1 + k), k))
    half = jnp.where(core == 0, sent[:, :HD], sent[:, HD:])
    far = send(half, lambda m, z, k: (m, z ^ 3, k)).astype(jnp.float32)
    zero = jnp.zeros_like(far)
    spread = jnp.concatenate(
        [jnp.where(core == 0, far, zero), jnp.where(core == 0, zero, far)], axis=1
    )
    mine = jnp.where(core == 0, sent.astype(jnp.float32), 0.0) + near.astype(jnp.float32) + spread
    if beside is not None:
        mine = jnp.concatenate([mine, beside], axis=1)
    return mine, core_swap(mine)


def split_high_low(value):
    high = value.astype(jnp.bfloat16)
    return high, (value - high.astype(jnp.float32)).astype(jnp.bfloat16)


def iota(shape, dimension):
    return lax.broadcasted_iota(jnp.int32, shape, dimension)


def one_hot(condition):
    return condition.astype(jnp.float32).astype(jnp.bfloat16)


def pooling_of(segments):
    return one_hot(iota((SEQS, segments.shape[1]), 0) == segments)


def lengths_of(segments):
    return jnp.sum(
        (iota((SEQS, segments.shape[1]), 0) == segments).astype(jnp.float32), axis=1, keepdims=True
    )


def here():
    return lax.axis_index("member"), lax.axis_index("shard")


def local_call(kernel, outputs, *operands):
    vmem = pl.BlockSpec(memory_space=pltpu.VMEM)
    return pl.pallas_call(
        kernel,
        out_shape=[jax.ShapeDtypeStruct(shape, dtype) for shape, dtype in outputs],
        in_specs=[vmem] * len(operands),
        out_specs=[vmem] * len(outputs),
        compiler_params=pltpu.CompilerParams(vmem_limit_bytes=KERNEL_VMEM),
    )(*operands)


def prepare_kernel(
    segment_ids, norm_gain, reward_weight, weight, trunk,
    segments_out, gain_out, weight_out, trunk_out, head_weight, sems,
):
    place = here()
    width = gain_out.shape[1]
    start = pl.multiple_of(place[1] % 2 * width, width)
    copies = [
        pltpu.make_async_copy(weight, weight_out, sems.at[0]),
        pltpu.make_async_copy(segment_ids, segments_out, sems.at[1]),
        pltpu.make_async_copy(norm_gain.at[:, pl.ds(start, width)], gain_out, sems.at[2]),
        pltpu.make_async_copy(reward_weight.at[:, pl.ds(start, width)], head_weight, sems.at[3]),
        pltpu.make_async_copy(trunk, trunk_out, sems.at[4]),
    ]
    for copy in copies:
        copy.start()
    for copy in copies:
        copy.wait()
    gain_out[...] = gain_out[...] * head_weight[...]


def prepare(segments, norm_gain, reward_weight, weight, trunk):
    width = norm_gain.shape[1] // 2
    return pl.pallas_call(
        prepare_kernel,
        out_shape=[
            jax.ShapeDtypeStruct(segments.shape, segments.dtype),
            jax.ShapeDtypeStruct((1, width), norm_gain.dtype),
            jax.ShapeDtypeStruct(weight.shape, weight.dtype),
            jax.ShapeDtypeStruct(trunk.shape, trunk.dtype),
        ],
        in_specs=[pl.BlockSpec(memory_space=pl.ANY)] * 5,
        out_specs=[pl.BlockSpec(memory_space=pltpu.VMEM)] * 4,
        scratch_shapes=[
            pltpu.VMEM((1, width), reward_weight.dtype),
            pltpu.SemaphoreType.DMA((5,)),
        ],
        compiler_params=pltpu.CompilerParams(vmem_limit_bytes=KERNEL_VMEM),
    )(segments, norm_gain, reward_weight, weight, trunk)


def stack_kernel(*refs):
    place = here()
    pieces, out, sems = refs[:-2], refs[-2], refs[-1]
    rows = pieces[0].shape[0]
    copies = []
    for step, ref in enumerate(pieces):
        start = pl.multiple_of(((place[1] // 2) ^ step) * rows, rows)
        copies.append(pltpu.make_async_copy(ref, out.at[pl.ds(start, rows), :], sems.at[step]))
    for copy in copies:
        copy.start()
    for copy in copies:
        copy.wait()


def stack_rows(blocks):
    rows, width = blocks[0].shape
    return pl.pallas_call(
        stack_kernel,
        out_shape=jax.ShapeDtypeStruct((len(blocks) * rows, width), blocks[0].dtype),
        in_specs=[pl.BlockSpec(memory_space=pl.ANY)] * len(blocks),
        out_specs=pl.BlockSpec(memory_space=pltpu.VMEM),
        scratch_shapes=[pltpu.SemaphoreType.DMA((len(blocks),))],
        compiler_params=pltpu.CompilerParams(vmem_limit_bytes=KERNEL_VMEM),
    )(*blocks)


def kv_columns_kernel(own, other, out):
    place = here()
    width = out.shape[1]
    rows = own.shape[0] // 4
    core = place[1] % 2
    start = pl.multiple_of(place[1] // 2 % 2 * width, width)
    for source, side in ((own, core), (other, 1 - core)):
        for step in range(4):
            to = pl.multiple_of((2 * step + side) * rows, rows)
            out[pl.ds(to, rows), :] = source[step * rows : (step + 1) * rows, pl.ds(start, width)]


def query_kernel(own, other, weight, out):
    place = here()
    rows = own.shape[0] // 4
    core = place[1] % 2
    for source, side in ((own, core), (other, 1 - core)):
        part = matmul(source[...], weight[...])
        for step in range(4):
            to = pl.multiple_of((2 * step + side) * rows, rows)
            out[pl.ds(to, rows), :] = part[step * rows : (step + 1) * rows]


def kv_kernel(segments, first, second, weight, out, pooled):
    place = here()
    far = (place[1] // 4) ^ (place[0] % 2)
    columns = jnp.where(far == 0, first[...], second[...])
    out[...] = matmul(columns, weight[...])
    pooled[...] = matmul(pooling_of(segments[...]), columns) / lengths_of(segments[...])


def forward_kernel(
    segments, mine, swapped, pooled, out_own, out_other, gain,
    queries_out, kv_out, attention_out, capped_out, message,
):
    bf16 = jnp.bfloat16
    place = here()
    core, height = place[1] % 2, place[1] // 2
    queries = (mine[:, 2 * HD :] + swapped[:, 2 * HD :]).astype(bf16)
    kv_values = (mine[:, : 2 * HD] + swapped[:, : 2 * HD]).astype(bf16)
    queries_out[...] = queries
    kv_out[...] = kv_values
    keys, values = kv_values[:, :HD], kv_values[:, HD:]
    pooling = pooling_of(segments[...])
    lengths = lengths_of(segments[...])
    tokens = pooling.shape[1]
    same = matmul_tn(pooling, pooling) > 0.5
    allowed = same & (iota((tokens, tokens), 1) <= iota((tokens, tokens), 0))
    raw_scores = matmul_nt(queries, keys) * (1.0 / math.sqrt(HD))
    capped = softcap_limit * jnp.tanh(raw_scores / softcap_limit)
    weights_exp = jnp.where(allowed, jnp.exp(capped), 0.0)
    attention = weights_exp / jnp.sum(weights_exp, axis=1, keepdims=True)
    attention_out[...] = attention
    capped_out[...] = capped
    attended = matmul(attention.astype(bf16), values).astype(bf16)
    seq_mean = (matmul(pooling, attended) / lengths).astype(bf16)
    half = out_own.shape[0]
    low, high = seq_mean[:, :half], seq_mean[:, half:]
    part = matmul(jnp.where(core == 0, low, high), out_own[...]) + matmul(
        jnp.where(core == 0, high, low), out_other[...]
    )
    width = pooled.shape[1]
    part = jnp.concatenate(
        [
            part[:, n * width : (n + 1) * width] + jnp.where(height == n, pooled[...], 0.0)
            for n in range(part.shape[1] // width)
        ],
        axis=1,
    )
    product_high, product_low = split_high_low(jnp.sum(part * gain[...], axis=1, keepdims=True))
    lane = iota((SEQS, HD), 1)
    message[:, : part.shape[1]] = part.astype(bf16)
    message[:, part.shape[1] :] = jnp.where(
        lane == 0,
        product_high.astype(jnp.float32),
        jnp.where(lane == 1, product_low.astype(jnp.float32), 0.0),
    ).astype(bf16)


def stats_kernel(
    first, second, third, fourth, out_own, out_other, gain, hidden_out, report
):
    core = here()[1] % 2
    half_width = hidden_out.shape[1]
    f32 = jnp.float32
    total = (first[...].astype(f32) + second[...].astype(f32)) + (
        third[...].astype(f32) + fourth[...].astype(f32)
    )
    hidden = total[:, :half_width]
    hidden_out[...] = hidden
    stacked = jnp.concatenate([hidden, jnp.broadcast_to(gain[...], hidden.shape)], axis=0)
    stacked = stacked.astype(jnp.bfloat16)
    along_own = matmul_nt(stacked, out_own[...])
    along_other = matmul_nt(stacked, out_other[...])
    half = along_own.shape[1]
    report[: 2 * SEQS, :half] = jnp.where(core == 0, along_own, along_other)
    report[: 2 * SEQS, half:] = jnp.where(core == 0, along_other, along_own)
    squares = jnp.sum(hidden * hidden, axis=1, keepdims=True)
    products = total[:, half_width : half_width + 1] + total[:, half_width + 1 : half_width + 2]
    lane = iota((SEQS, HD), 1)
    report[2 * SEQS :, :] = jnp.where(lane == 0, squares, jnp.where(lane == 1, products, 0.0))


def member_order(place, tokens):
    rows = tokens // 4
    position = iota((tokens, tokens), 0)
    token = rows * (place[0] ^ (position // rows)) + position % rows
    return one_hot(iota((tokens, tokens), 1) == token)


def backward_kernel(
    pairs, segments, mine, swapped, queries, kv_values, attention, capped,
    query_grad, kv_grad, rewards_out, factors, *, full_width,
):
    bf16 = jnp.bfloat16
    width = full_width
    report = mine[...] + swapped[...]
    hidden_along, gain_along = report[:SEQS], report[SEQS : 2 * SEQS]
    square_sum, product_sum = report[2 * SEQS :, 0:1], report[2 * SEQS :, 1:2]
    pooling = pooling_of(segments[...])
    lengths = lengths_of(segments[...])
    inverse_rms = lax.rsqrt(square_sum / width + norm_eps)
    rewards = product_sum * inverse_rms
    diagonal = iota((SEQS, SEQS), 0) == iota((SEQS, SEQS), 1)
    rewards_row = jnp.sum(jnp.where(diagonal, rewards, 0.0), axis=0, keepdims=True)
    rewards_out[...] = rewards_row
    signs = pairs[...]
    margin = jnp.sum(signs * rewards_row, axis=1, keepdims=True)
    pair_slope = loss_scale / (1.0 + jnp.exp(margin))
    grad_row = -jnp.sum(signs * pair_slope, axis=0, keepdims=True)
    reward_grad = jnp.sum(jnp.where(diagonal, grad_row, 0.0), axis=1, keepdims=True)
    gain_factor = inverse_rms * reward_grad / lengths
    hidden_factor = inverse_rms * inverse_rms * inverse_rms * (
        reward_grad * product_sum / width
    ) / lengths
    factors[0] = jnp.broadcast_to(gain_factor, (SEQS, HD))
    factors[1] = jnp.broadcast_to(hidden_factor, (SEQS, HD))
    mean_grad = (gain_factor * gain_along - hidden_factor * hidden_along).astype(bf16)
    out_grad = matmul_tn(pooling, mean_grad).astype(bf16)
    keys, values = kv_values[:, :HD], kv_values[:, HD:]
    attn = attention[...]
    prob_grad = matmul_nt(out_grad, values)
    score_grad = attn * (prob_grad - jnp.sum(attn * prob_grad, axis=1, keepdims=True))
    ratio = capped[...] / softcap_limit
    raw_grad = (score_grad * (1.0 - ratio * ratio) * (1.0 / math.sqrt(HD))).astype(bf16)
    order = member_order(here(), attn.shape[0])
    query_grad[...] = matmul(order, matmul(raw_grad, keys).astype(bf16)).astype(bf16)
    kv_grad[:, :HD] = matmul_tn(raw_grad, queries[...])
    kv_grad[:, HD:] = matmul_tn(attn.astype(bf16), out_grad)


def far_kernel(grad, weight, far):
    place = here()
    width = far.shape[1] // 3
    for step in (1, 2, 3):
        start = pl.multiple_of(((place[1] // 2) ^ step) * width, width)
        far[:, (step - 1) * width : step * width] = matmul_nt(
            grad[...], weight[pl.ds(start, width), :]
        ).astype(far.dtype)


def near_kernel(
    segments, grad, weight, kv_mine, kv_swapped, kv_weight, hidden, gain, factors, near
):
    bf16 = jnp.bfloat16
    place = here()
    width = near.shape[1]
    start = pl.multiple_of(place[1] // 2 * width, width)
    order = member_order(place, near.shape[0])
    kv_grad = (kv_mine[...] + kv_swapped[...]).astype(bf16)
    kv_turned = matmul(order, kv_grad).astype(bf16)
    seq_turned = matmul_nt(order, pooling_of(segments[...])).astype(bf16)
    gain_block = gain[:, pl.ds(start, width)]
    high, low = split_high_low(
        factors[0][:, 0:1] * gain_block - factors[1][:, 0:1] * hidden[:, pl.ds(start, width)]
    )
    near[...] = (
        matmul_nt(grad[...], weight[pl.ds(start, width), :])
        + matmul_nt(kv_turned, kv_weight[...])
        + matmul(seq_turned, high)
        + matmul(seq_turned, low)
    ).astype(bf16)


def sum_of(own, first, second, third, start, width):
    f32 = jnp.float32
    rows = first.shape[0]
    return (
        (own[:rows, start : start + width].astype(f32) + first[:, start : start + width].astype(f32))
        + (
            second[:, start : start + width].astype(f32)
            + third[:, start : start + width].astype(f32)
        )
    ).astype(own.dtype)


def place_of(step, width):
    return pl.multiple_of(((here()[1] // 2) ^ step) % 2 * width, width)


def far_sum_kernel(own, first, second, third, one, two):
    width = one.shape[1]
    one[...] = sum_of(own, first, second, third, 0, width)
    for step in (2, 3):
        two[:, pl.ds(place_of(step, width), width)] = sum_of(
            own, first, second, third, (step - 1) * width, width
        )


def near_sum_kernel(own, first, second, third, one, two):
    width = one.shape[1]
    two[:, pl.ds(place_of(0, width), width)] = sum_of(own, first, second, third, 0, width)
    two[:, pl.ds(place_of(1, width), width)] = one[...]


def merge_kernel(first, second, kept, given):
    width = kept.shape[1]
    core = here()[1] % 2
    for out, side in ((kept, core), (given, 1 - core)):
        columns = pl.ds(pl.multiple_of(side * width, width), width)
        out[...] = first[:, columns].astype(jnp.float32) + second[:, columns].astype(jnp.float32)


def fast_device(
    trunk_out, segment_ids, pair_order, w_query, w_key_value, w_out, norm_gain, reward_weight
):
    bf16, f32 = jnp.bfloat16, jnp.float32
    member = lax.axis_index("member")
    shard = lax.axis_index("shard")
    core = shard % 2
    col = member % 2
    local_width = trunk_out.shape[1]
    tokens = segment_ids.shape[0]
    half_width = w_query.shape[2]
    block_width = w_key_value.shape[2]
    member_rows = tokens // 4
    query_piece = w_query[0, 0]
    kv_piece = w_key_value[0, 0]

    stack = [send(trunk_out, lambda m, z, k, d=d: (m, z ^ d, k)) for d in (1, 2, 3)]

    cuts = [
        lax.dynamic_slice_in_dim(query_piece, (col ^ r) * local_width, local_width, 0)
        for r in (0, 1)
    ]
    weights = [
        send(cuts[r], lambda m, z, k, r=r: (2 * k + ((m % 2) ^ r), z, m // 2))
        for r in (0, 1)
    ]

    segments, gain, kv_weight, trunk_near = prepare(
        segment_ids[None, :], norm_gain, reward_weight, kv_piece, trunk_out
    )
    column_own = stack_rows([trunk_near] + stack)
    column_other = core_swap(column_own)
    block_shape = ((tokens, block_width), bf16)
    (kv_sent,) = local_call(kv_columns_kernel, [block_shape], column_own, column_other)
    kv_got = [
        send(
            kv_sent,
            lambda m, z, k, r=r: (2 * k + ((m % 2) ^ r), z, m // 2) if m % 2 == z // 2 else None,
        )
        for r in (0, 1)
    ]
    head_shape = ((tokens, HD), f32)
    query_parts = [
        local_call(query_kernel, [head_shape], column_own, column_other, weights[r])[0]
        for r in (0, 1)
    ]
    query_got = [
        send(part, lambda m, z, k, r=r: (2 * k + ((m % 2) ^ r), z, m // 2))
        for r, part in enumerate(query_parts)
    ]
    kv_part, pooled = local_call(
        kv_kernel,
        [((tokens, 2 * HD), f32), ((SEQS, block_width), f32)],
        segments,
        *kv_got,
        kv_weight,
    )
    kv_part = kv_part + core_swap(kv_part)
    mine, swapped = height_total(kv_part, core, jnp.float16, query_got[0] + query_got[1])

    out_rows, _ = lax.optimization_barrier((w_out[0], kv_part))
    out_own = lax.dynamic_slice_in_dim(out_rows, core * half_width, half_width, 1)
    out_other = core_swap(
        lax.dynamic_slice_in_dim(out_rows, (1 - core) * half_width, half_width, 1)
    )

    queries, kv_values, attention, capped, message = local_call(
        forward_kernel,
        [
            ((tokens, HD), bf16),
            ((tokens, 2 * HD), bf16),
            ((tokens, tokens), f32),
            ((tokens, tokens), f32),
            ((SEQS, half_width + HD), bf16),
        ],
        segments, mine, swapped, pooled, out_own, out_other, gain,
    )
    others = [send(message, lambda m, z, k, d=d: (m, z ^ d, k)) for d in (1, 2, 3)]
    hidden, report = local_call(
        stats_kernel,
        [((SEQS, half_width), f32), ((3 * SEQS, HD), f32)],
        message, *others, out_own, out_other, gain,
    )
    seq_ids = jnp.arange(SEQS)[None, :]
    pairs = (pair_order[0::2][:, None] == seq_ids).astype(f32) - (
        pair_order[1::2][:, None] == seq_ids
    ).astype(f32)
    pairs = jnp.concatenate([pairs, jnp.zeros_like(pairs)], axis=0)
    query_grad, kv_grad, rewards, factors = local_call(
        functools.partial(backward_kernel, full_width=float(2 * half_width)),
        [
            ((tokens, HD), bf16),
            ((tokens, 2 * HD), f32),
            ((1, SEQS), f32),
            ((2, SEQS, HD), f32),
        ],
        pairs, segments, report, core_swap(report), queries, kv_values, attention, capped,
    )

    kv_mine, kv_swapped = height_total(kv_grad, core, bf16)
    (far_grad,) = local_call(
        far_kernel, [((tokens, 3 * block_width), bf16)], query_grad, query_piece
    )
    far_got = [
        send(far_grad[d * member_rows : (d + 1) * member_rows], lambda m, z, k, d=d: (m ^ d, z, k))
        for d in (1, 2, 3)
    ]
    (near_grad,) = local_call(
        near_kernel,
        [block_shape],
        segments, query_grad, query_piece, kv_mine, kv_swapped, kv_weight, hidden, gain,
        factors,
    )
    near_got = [
        send(near_grad[d * member_rows : (d + 1) * member_rows], lambda m, z, k, d=d: (m ^ d, z, k))
        for d in (1, 2, 3)
    ]
    sum_shape = ((member_rows, block_width), bf16)
    pair_shape = ((member_rows, 2 * block_width), bf16)
    far_one, far_pair = local_call(far_sum_kernel, [sum_shape, pair_shape], far_grad, *far_got)
    far_part = send(far_pair, lambda m, z, k: (m, 2 * k + 1 - z // 2, z % 2))
    (near_pair,) = local_call(near_sum_kernel, [pair_shape], near_grad, *near_got, far_one)
    near_part = send(near_pair, lambda m, z, k: (m, 2 * k + z // 2, z % 2))
    kept, given = local_call(
        merge_kernel, [((member_rows, block_width), f32)] * 2, far_part, near_part
    )
    total = kept + core_swap(given)
    return (total, rewards)


def solution(mesh):
    fast = dict(mesh.shape) == {"member": 4, "shard": 8}
    placed = (
        P("shard", "member"),
        P(),
        P(),
        P("member", "shard", None, None),
        P("member", "shard", None, None),
        P("member", "shard", None),
        P("member", None),
        P("member", None),
    )
    return jax.shard_map(
        fast_device if fast else general_device,
        mesh=mesh,
        in_specs=placed,
        out_specs=(P("member", "shard"), P("member", None)),
        check_vma=False,
    )
```

```python
import functools
import math

import jax
import jax.numpy as jnp
from jax import lax
from jax.experimental import pallas as pl
from jax.experimental.pallas import tpu as pltpu
from jax.sharding import PartitionSpec as P


HD = 128
SEQS = 8


KERNEL_VMEM = 8 << 20
softcap_limit = 20.0
loss_scale = 256.0
norm_eps = 1e-05


def from_partner(block, axis, stride):
    count = lax.axis_size(axis)
    route = []
    for low in range(count):
        high = low | 1 << stride
        if high != low and high < count:
            route += [(low, high), (high, low)]
    return lax.ppermute(block, axis, route)


def partner_swap(values, bit_number):
    return from_partner(values, "shard", bit_number)


def group_total(values, bit_list):
    for bit_number in bit_list:
        values = values + partner_swap(values, bit_number)
    return values


def pair_join(own_part, other_part, pair_side, join_axis):
    first_part = jnp.where(pair_side == 0, own_part, other_part)
    second_part = jnp.where(pair_side == 0, other_part, own_part)
    return jnp.concatenate([first_part, second_part], axis=join_axis)


def general_device(
    trunk_out, segment_ids, pair_order, w_query, w_key_value, w_out, norm_gain, reward_weight
):
    n_shard = lax.axis_size("shard")
    query_heads = n_shard // 2
    kv_count = max(1, query_heads // 8)
    group_size = query_heads // kv_count
    shard_index = lax.axis_index("shard")
    pair_side = shard_index % 2
    head_index = shard_index // 2
    block_index = shard_index % (2 * group_size) // 2
    local_rows, _ = trunk_out.shape
    features = lax.all_gather(trunk_out, "member", axis=1, tiled=True)
    gathered = lax.all_gather(features, "shard", axis=0, tiled=True)
    tok_count, model_width = gathered.shape
    half_width = model_width // 2
    half_rows = tok_count // 2
    half_head = HD // 2
    row_block = half_width // group_size
    scale_factor = 1.0 / math.sqrt(HD)
    group_bits = list(range((2 * group_size).bit_length() - 1))
    query_piece = w_query[0, 0]
    kv_piece = w_key_value[0, 0]
    out_rows = w_out[0]
    gain_vector = norm_gain[0]
    head_weight = reward_weight[0]
    positions = jnp.arange(tok_count)
    own_start = pair_side * half_rows
    own_positions = own_start + jnp.arange(half_rows)
    own_segments = lax.dynamic_slice_in_dim(segment_ids, own_start, half_rows, 0)
    allowed = (own_segments[:, None] == segment_ids[None, :]) & (
        positions[None, :] <= own_positions[:, None]
    )
    member_of = jnp.arange(SEQS)[:, None] == segment_ids[None, :]
    pooling = member_of.astype(jnp.bfloat16)
    lengths = jnp.sum(member_of.astype(jnp.float32), axis=1)
    own_pooling = lax.dynamic_slice_in_dim(pooling, own_start, half_rows, 1)
    half_features = lax.dynamic_slice_in_dim(gathered, pair_side * half_width, half_width, 1)
    query_partial = jnp.dot(half_features, query_piece, preferred_element_type=jnp.float32)
    kept_rows = lax.dynamic_slice_in_dim(query_partial, own_start, half_rows, 0)
    sent_rows = lax.dynamic_slice_in_dim(query_partial, half_rows - own_start, half_rows, 0)
    queries = (kept_rows + partner_swap(sent_rows, 0)).astype(jnp.bfloat16)
    kv_features = lax.dynamic_slice_in_dim(half_features, block_index * row_block, row_block, 1)
    kv_values = group_total(
        jnp.dot(kv_features, kv_piece, preferred_element_type=jnp.float32), group_bits
    ).astype(jnp.bfloat16)
    key_full = kv_values[:, :HD]
    value_full = kv_values[:, HD:]
    raw_scores = (
        jnp.einsum("td,sd->ts", queries, key_full, preferred_element_type=jnp.float32)
        * scale_factor
    )
    capped = softcap_limit * jnp.tanh(raw_scores / softcap_limit)
    weights_exp = jnp.where(allowed, jnp.exp(capped), 0.0)
    attention = weights_exp / jnp.sum(weights_exp, axis=1, keepdims=True)
    attention_low = attention.astype(jnp.bfloat16)
    attended = jnp.dot(attention_low, value_full, preferred_element_type=jnp.float32).astype(
        jnp.bfloat16
    )
    seq_part = jnp.dot(own_pooling, attended, preferred_element_type=jnp.float32)
    seq_total = seq_part + partner_swap(seq_part, 0)
    seq_mean = (seq_total / lengths[:, None]).astype(jnp.bfloat16)
    own_dims = lax.dynamic_slice_in_dim(seq_mean, pair_side * half_head, half_head, 1)
    head_part = jnp.dot(own_dims, out_rows, preferred_element_type=jnp.float32)
    pooled_attn = lax.psum(head_part, "shard")
    pooled_input = jnp.dot(pooling, gathered, preferred_element_type=jnp.float32) / lengths[:, None]
    hidden = pooled_input + pooled_attn
    inverse_rms = lax.rsqrt(jnp.mean(hidden * hidden, axis=1) + norm_eps)
    normed = hidden * inverse_rms[:, None] * gain_vector
    rewards = jnp.sum(normed * head_weight, axis=1)
    seq_ids = jnp.arange(SEQS)
    chosen = (pair_order[0::2][:, None] == seq_ids[None, :]).astype(jnp.float32)
    rejected = (pair_order[1::2][:, None] == seq_ids[None, :]).astype(jnp.float32)
    margin = jnp.sum(chosen * rewards, axis=1) - jnp.sum(rejected * rewards, axis=1)
    pair_slope = loss_scale * jax.nn.sigmoid(-margin)
    reward_grad = jnp.sum(rejected * pair_slope[:, None], axis=0) - jnp.sum(
        chosen * pair_slope[:, None], axis=0
    )
    scaled_grad = reward_grad[:, None] * head_weight * gain_vector
    hidden_grad = inverse_rms[:, None] * (
        scaled_grad
        - hidden * (inverse_rms**2)[:, None] * jnp.mean(hidden * scaled_grad, axis=1, keepdims=True)
    )
    per_token = hidden_grad / lengths[:, None]
    grad_low = hidden_grad.astype(jnp.bfloat16)
    grad_dims = (
        jnp.einsum("jd,ed->je", grad_low, out_rows, preferred_element_type=jnp.float32)
        / lengths[:, None]
    )
    mean_grad = pair_join(grad_dims, partner_swap(grad_dims, 0), pair_side, 1)
    out_grad = jnp.take(mean_grad, own_segments, axis=0).astype(jnp.bfloat16)
    prob_grad = jnp.einsum("td,sd->ts", out_grad, value_full, preferred_element_type=jnp.float32)
    score_grad = attention * (prob_grad - jnp.sum(attention * prob_grad, axis=1, keepdims=True))
    raw_grad = (score_grad * (1.0 - (capped / softcap_limit) ** 2) * scale_factor).astype(
        jnp.bfloat16
    )
    query_grad = jnp.dot(raw_grad, key_full, preferred_element_type=jnp.float32).astype(
        jnp.bfloat16
    )
    key_grad = jnp.einsum("ts,td->sd", raw_grad, queries, preferred_element_type=jnp.float32)
    value_grad = jnp.einsum(
        "ts,td->sd", attention_low, out_grad, preferred_element_type=jnp.float32
    )
    kv_grad = group_total(jnp.concatenate([key_grad, value_grad], axis=1), group_bits).astype(
        jnp.bfloat16
    )
    query_wire = lax.optimization_barrier(query_grad).astype(jnp.float32)
    query_all = pair_join(
        query_grad, partner_swap(query_wire, 0).astype(jnp.bfloat16), pair_side, 0
    )
    grad_half = jnp.einsum("td,rd->tr", query_all, query_piece, preferred_element_type=jnp.float32)
    kv_term = jnp.einsum("te,re->tr", kv_grad, kv_piece, preferred_element_type=jnp.float32)
    start_col = block_index * row_block
    grad_half = lax.dynamic_update_slice_in_dim(
        grad_half,
        lax.dynamic_slice_in_dim(grad_half, start_col, row_block, 1) + kv_term,
        start_col,
        1,
    )
    pair_rows = 2 * local_rows
    start_row = head_index * pair_rows
    pair_segments = lax.dynamic_slice_in_dim(segment_ids, start_row, pair_rows, 0)
    token_half = lax.dynamic_slice_in_dim(per_token, pair_side * half_width, half_width, 1)
    direct = jnp.take(token_half, pair_segments, axis=0)
    grad_half = lax.dynamic_update_slice_in_dim(
        grad_half,
        lax.dynamic_slice_in_dim(grad_half, start_row, pair_rows, 0) + direct,
        start_row,
        0,
    )
    by_member = lax.psum_scatter(grad_half, "member", scatter_dimension=0, tiled=True)
    member_rows = by_member.shape[0]
    placed = lax.dynamic_update_slice_in_dim(
        jnp.zeros((member_rows, model_width), jnp.float32), by_member, pair_side * half_width, 1
    )
    trunk_grad = lax.psum_scatter(placed, "shard", scatter_dimension=1, tiled=True)
    return (trunk_grad, rewards[None])


def route_pairs(target):
    pairs = []
    for member in range(4):
        for height in range(4):
            for core in range(2):
                to = target(member, height, core)
                if to is not None:
                    pairs.append((member * 8 + height * 2 + core, to[0] * 8 + to[1] * 2 + to[2]))
    return pairs


def send(block, target):
    return lax.ppermute(block, ("member", "shard"), route_pairs(target))


def core_swap(block):
    return send(block, lambda m, z, k: (m, z, 1 - k))


def matmul(left, right):
    return jnp.dot(left, right, preferred_element_type=jnp.float32)


def matmul_nt(left, right):
    return lax.dot_general(
        left, right, (((1,), (1,)), ((), ())), preferred_element_type=jnp.float32
    )


def matmul_tn(left, right):
    return lax.dot_general(
        left, right, (((0,), (0,)), ((), ())), preferred_element_type=jnp.float32
    )


def height_total(block, core, wire, beside=None):
    sent = block.astype(wire)
    near = send(sent, lambda m, z, k: (m, z ^ (1 + k), k))
    half = jnp.where(core == 0, sent[:, :HD], sent[:, HD:])
    far = send(half, lambda m, z, k: (m, z ^ 3, k)).astype(jnp.float32)
    zero = jnp.zeros_like(far)
    spread = jnp.concatenate(
        [jnp.where(core == 0, far, zero), jnp.where(core == 0, zero, far)], axis=1
    )
    mine = jnp.where(core == 0, sent.astype(jnp.float32), 0.0) + near.astype(jnp.float32) + spread
    if beside is not None:
        mine = jnp.concatenate([mine, beside], axis=1)
    return mine, core_swap(mine)


def split_high_low(value):
    high = value.astype(jnp.bfloat16)
    return high, (value - high.astype(jnp.float32)).astype(jnp.bfloat16)


def iota(shape, dimension):
    return lax.broadcasted_iota(jnp.int32, shape, dimension)


def one_hot(condition):
    return condition.astype(jnp.float32).astype(jnp.bfloat16)


def pooling_of(segments):
    return one_hot(iota((SEQS, segments.shape[1]), 0) == segments)


def lengths_of(segments):
    return jnp.sum(
        (iota((SEQS, segments.shape[1]), 0) == segments).astype(jnp.float32), axis=1, keepdims=True
    )


def here():
    return lax.axis_index("member"), lax.axis_index("shard")


def local_call(kernel, outputs, *operands):
    vmem = pl.BlockSpec(memory_space=pltpu.VMEM)
    return pl.pallas_call(
        kernel,
        out_shape=[jax.ShapeDtypeStruct(shape, dtype) for shape, dtype in outputs],
        in_specs=[vmem] * len(operands),
        out_specs=[vmem] * len(outputs),
        compiler_params=pltpu.CompilerParams(vmem_limit_bytes=KERNEL_VMEM),
    )(*operands)


def prepare_kernel(
    segment_ids, norm_gain, reward_weight, weight, trunk,
    segments_out, gain_out, weight_out, trunk_out, head_weight, sems,
):
    place = here()
    width = gain_out.shape[1]
    start = pl.multiple_of(place[1] % 2 * width, width)
    copies = [
        pltpu.make_async_copy(weight, weight_out, sems.at[0]),
        pltpu.make_async_copy(segment_ids, segments_out, sems.at[1]),
        pltpu.make_async_copy(norm_gain.at[:, pl.ds(start, width)], gain_out, sems.at[2]),
        pltpu.make_async_copy(reward_weight.at[:, pl.ds(start, width)], head_weight, sems.at[3]),
        pltpu.make_async_copy(trunk, trunk_out, sems.at[4]),
    ]
    for copy in copies:
        copy.start()
    for copy in copies:
        copy.wait()
    gain_out[...] = gain_out[...] * head_weight[...]


def prepare(segments, norm_gain, reward_weight, weight, trunk):
    width = norm_gain.shape[1] // 2
    return pl.pallas_call(
        prepare_kernel,
        out_shape=[
            jax.ShapeDtypeStruct(segments.shape, segments.dtype),
            jax.ShapeDtypeStruct((1, width), norm_gain.dtype),
            jax.ShapeDtypeStruct(weight.shape, weight.dtype),
            jax.ShapeDtypeStruct(trunk.shape, trunk.dtype),
        ],
        in_specs=[pl.BlockSpec(memory_space=pl.ANY)] * 5,
        out_specs=[pl.BlockSpec(memory_space=pltpu.VMEM)] * 4,
        scratch_shapes=[
            pltpu.VMEM((1, width), reward_weight.dtype),
            pltpu.SemaphoreType.DMA((5,)),
        ],
        compiler_params=pltpu.CompilerParams(vmem_limit_bytes=KERNEL_VMEM),
    )(segments, norm_gain, reward_weight, weight, trunk)


def stack_kernel(*refs):
    place = here()
    pieces, out, sems = refs[:-2], refs[-2], refs[-1]
    rows = pieces[0].shape[0]
    copies = []
    for step, ref in enumerate(pieces):
        start = pl.multiple_of(((place[1] // 2) ^ step) * rows, rows)
        copies.append(pltpu.make_async_copy(ref, out.at[pl.ds(start, rows), :], sems.at[step]))
    for copy in copies:
        copy.start()
    for copy in copies:
        copy.wait()


def stack_rows(blocks):
    rows, width = blocks[0].shape
    return pl.pallas_call(
        stack_kernel,
        out_shape=jax.ShapeDtypeStruct((len(blocks) * rows, width), blocks[0].dtype),
        in_specs=[pl.BlockSpec(memory_space=pl.ANY)] * len(blocks),
        out_specs=pl.BlockSpec(memory_space=pltpu.VMEM),
        scratch_shapes=[pltpu.SemaphoreType.DMA((len(blocks),))],
        compiler_params=pltpu.CompilerParams(vmem_limit_bytes=KERNEL_VMEM),
    )(*blocks)


def kv_columns_kernel(own, other, out):
    place = here()
    width = out.shape[1]
    rows = own.shape[0] // 4
    core = place[1] % 2
    start = pl.multiple_of(place[1] // 2 % 2 * width, width)
    for source, side in ((own, core), (other, 1 - core)):
        for step in range(4):
            to = pl.multiple_of((2 * step + side) * rows, rows)
            out[pl.ds(to, rows), :] = source[step * rows : (step + 1) * rows, pl.ds(start, width)]


def query_kernel(own, other, weight, out):
    place = here()
    rows = own.shape[0] // 4
    core = place[1] % 2
    for source, side in ((own, core), (other, 1 - core)):
        part = matmul(source[...], weight[...])
        for step in range(4):
            to = pl.multiple_of((2 * step + side) * rows, rows)
            out[pl.ds(to, rows), :] = part[step * rows : (step + 1) * rows]


def kv_kernel(segments, first, second, weight, out, pooled):
    place = here()
    far = (place[1] // 4) ^ (place[0] % 2)
    columns = jnp.where(far == 0, first[...], second[...])
    out[...] = matmul(columns, weight[...])
    pooled[...] = matmul(pooling_of(segments[...]), columns) / lengths_of(segments[...])


def forward_kernel(
    segments, mine, swapped, pooled, out_own, out_other, gain,
    queries_out, kv_out, attention_out, capped_out, message,
):
    bf16 = jnp.bfloat16
    place = here()
    core, height = place[1] % 2, place[1] // 2
    queries = (mine[:, 2 * HD :] + swapped[:, 2 * HD :]).astype(bf16)
    kv_values = (mine[:, : 2 * HD] + swapped[:, : 2 * HD]).astype(bf16)
    queries_out[...] = queries
    kv_out[...] = kv_values
    keys, values = kv_values[:, :HD], kv_values[:, HD:]
    pooling = pooling_of(segments[...])
    lengths = lengths_of(segments[...])
    tokens = pooling.shape[1]
    same = matmul_tn(pooling, pooling) > 0.5
    allowed = same & (iota((tokens, tokens), 1) <= iota((tokens, tokens), 0))
    raw_scores = matmul_nt(queries, keys) * (1.0 / math.sqrt(HD))
    capped = softcap_limit * jnp.tanh(raw_scores / softcap_limit)
    weights_exp = jnp.where(allowed, jnp.exp(capped), 0.0)
    attention = weights_exp / jnp.sum(weights_exp, axis=1, keepdims=True)
    attention_out[...] = attention
    capped_out[...] = capped
    attended = matmul(attention.astype(bf16), values).astype(bf16)
    seq_mean = (matmul(pooling, attended) / lengths).astype(bf16)
    half = out_own.shape[0]
    low, high = seq_mean[:, :half], seq_mean[:, half:]
    part = matmul(jnp.where(core == 0, low, high), out_own[...]) + matmul(
        jnp.where(core == 0, high, low), out_other[...]
    )
    width = pooled.shape[1]
    part = jnp.concatenate(
        [
            part[:, n * width : (n + 1) * width] + jnp.where(height == n, pooled[...], 0.0)
            for n in range(part.shape[1] // width)
        ],
        axis=1,
    )
    product_high, product_low = split_high_low(jnp.sum(part * gain[...], axis=1, keepdims=True))
    lane = iota((SEQS, HD), 1)
    message[:, : part.shape[1]] = part.astype(bf16)
    message[:, part.shape[1] :] = jnp.where(
        lane == 0,
        product_high.astype(jnp.float32),
        jnp.where(lane == 1, product_low.astype(jnp.float32), 0.0),
    ).astype(bf16)


def stats_kernel(
    first, second, third, fourth, out_own, out_other, gain, hidden_out, report
):
    core = here()[1] % 2
    half_width = hidden_out.shape[1]
    f32 = jnp.float32
    total = (first[...].astype(f32) + second[...].astype(f32)) + (
        third[...].astype(f32) + fourth[...].astype(f32)
    )
    hidden = total[:, :half_width]
    hidden_out[...] = hidden
    stacked = jnp.concatenate([hidden, jnp.broadcast_to(gain[...], hidden.shape)], axis=0)
    stacked = stacked.astype(jnp.bfloat16)
    along_own = matmul_nt(stacked, out_own[...])
    along_other = matmul_nt(stacked, out_other[...])
    half = along_own.shape[1]
    report[: 2 * SEQS, :half] = jnp.where(core == 0, along_own, along_other)
    report[: 2 * SEQS, half:] = jnp.where(core == 0, along_other, along_own)
    squares = jnp.sum(hidden * hidden, axis=1, keepdims=True)
    products = total[:, half_width : half_width + 1] + total[:, half_width + 1 : half_width + 2]
    lane = iota((SEQS, HD), 1)
    report[2 * SEQS :, :] = jnp.where(lane == 0, squares, jnp.where(lane == 1, products, 0.0))


def member_order(place, tokens):
    rows = tokens // 4
    position = iota((tokens, tokens), 0)
    token = rows * (place[0] ^ (position // rows)) + position % rows
    return one_hot(iota((tokens, tokens), 1) == token)


def backward_kernel(
    pairs, segments, mine, swapped, queries, kv_values, attention, capped,
    query_grad, kv_grad, rewards_out, factors, *, full_width,
):
    bf16 = jnp.bfloat16
    width = full_width
    report = mine[...] + swapped[...]
    hidden_along, gain_along = report[:SEQS], report[SEQS : 2 * SEQS]
    square_sum, product_sum = report[2 * SEQS :, 0:1], report[2 * SEQS :, 1:2]
    pooling = pooling_of(segments[...])
    lengths = lengths_of(segments[...])
    inverse_rms = lax.rsqrt(square_sum / width + norm_eps)
    rewards = product_sum * inverse_rms
    diagonal = iota((SEQS, SEQS), 0) == iota((SEQS, SEQS), 1)
    rewards_row = jnp.sum(jnp.where(diagonal, rewards, 0.0), axis=0, keepdims=True)
    rewards_out[...] = rewards_row
    signs = pairs[...]
    margin = jnp.sum(signs * rewards_row, axis=1, keepdims=True)
    pair_slope = loss_scale / (1.0 + jnp.exp(margin))
    grad_row = -jnp.sum(signs * pair_slope, axis=0, keepdims=True)
    reward_grad = jnp.sum(jnp.where(diagonal, grad_row, 0.0), axis=1, keepdims=True)
    gain_factor = inverse_rms * reward_grad / lengths
    hidden_factor = inverse_rms * inverse_rms * inverse_rms * (
        reward_grad * product_sum / width
    ) / lengths
    factors[0] = jnp.broadcast_to(gain_factor, (SEQS, HD))
    factors[1] = jnp.broadcast_to(hidden_factor, (SEQS, HD))
    mean_grad = (gain_factor * gain_along - hidden_factor * hidden_along).astype(bf16)
    out_grad = matmul_tn(pooling, mean_grad).astype(bf16)
    keys, values = kv_values[:, :HD], kv_values[:, HD:]
    attn = attention[...]
    prob_grad = matmul_nt(out_grad, values)
    score_grad = attn * (prob_grad - jnp.sum(attn * prob_grad, axis=1, keepdims=True))
    ratio = capped[...] / softcap_limit
    raw_grad = (score_grad * (1.0 - ratio * ratio) * (1.0 / math.sqrt(HD))).astype(bf16)
    order = member_order(here(), attn.shape[0])
    query_grad[...] = matmul(order, matmul(raw_grad, keys).astype(bf16)).astype(bf16)
    kv_grad[:, :HD] = matmul_tn(raw_grad, queries[...])
    kv_grad[:, HD:] = matmul_tn(attn.astype(bf16), out_grad)


def far_kernel(grad, weight, far):
    place = here()
    width = far.shape[1] // 3
    for step in (1, 2, 3):
        start = pl.multiple_of(((place[1] // 2) ^ step) * width, width)
        far[:, (step - 1) * width : step * width] = matmul_nt(
            grad[...], weight[pl.ds(start, width), :]
        ).astype(far.dtype)


def near_kernel(
    segments, grad, weight, kv_mine, kv_swapped, kv_weight, hidden, gain, factors, near
):
    bf16 = jnp.bfloat16
    place = here()
    width = near.shape[1]
    start = pl.multiple_of(place[1] // 2 * width, width)
    order = member_order(place, near.shape[0])
    kv_grad = (kv_mine[...] + kv_swapped[...]).astype(bf16)
    kv_turned = matmul(order, kv_grad).astype(bf16)
    seq_turned = matmul_nt(order, pooling_of(segments[...])).astype(bf16)
    gain_block = gain[:, pl.ds(start, width)]
    high, low = split_high_low(
        factors[0][:, 0:1] * gain_block - factors[1][:, 0:1] * hidden[:, pl.ds(start, width)]
    )
    near[...] = (
        matmul_nt(grad[...], weight[pl.ds(start, width), :])
        + matmul_nt(kv_turned, kv_weight[...])
        + matmul(seq_turned, high)
        + matmul(seq_turned, low)
    ).astype(bf16)


def sum_of(own, first, second, third, start, width):
    f32 = jnp.float32
    rows = first.shape[0]
    return (
        (own[:rows, start : start + width].astype(f32) + first[:, start : start + width].astype(f32))
        + (
            second[:, start : start + width].astype(f32)
            + third[:, start : start + width].astype(f32)
        )
    ).astype(own.dtype)


def place_of(step, width):
    return pl.multiple_of(((here()[1] // 2) ^ step) % 2 * width, width)


def far_sum_kernel(own, first, second, third, one, two):
    width = one.shape[1]
    one[...] = sum_of(own, first, second, third, 0, width)
    for step in (2, 3):
        two[:, pl.ds(place_of(step, width), width)] = sum_of(
            own, first, second, third, (step - 1) * width, width
        )


def near_sum_kernel(own, first, second, third, one, two):
    width = one.shape[1]
    two[:, pl.ds(place_of(0, width), width)] = sum_of(own, first, second, third, 0, width)
    two[:, pl.ds(place_of(1, width), width)] = one[...]


def merge_kernel(first, second, kept, given):
    width = kept.shape[1]
    core = here()[1] % 2
    for out, side in ((kept, core), (given, 1 - core)):
        columns = pl.ds(pl.multiple_of(side * width, width), width)
        out[...] = (
            first[:, columns].astype(jnp.float32) + second[:, columns].astype(jnp.float32)
        ).astype(out.dtype)


def fast_device(
    trunk_out, segment_ids, pair_order, w_query, w_key_value, w_out, norm_gain, reward_weight
):
    bf16, f32 = jnp.bfloat16, jnp.float32
    member = lax.axis_index("member")
    shard = lax.axis_index("shard")
    core = shard % 2
    col = member % 2
    local_width = trunk_out.shape[1]
    tokens = segment_ids.shape[0]
    half_width = w_query.shape[2]
    block_width = w_key_value.shape[2]
    member_rows = tokens // 4
    query_piece = w_query[0, 0]
    kv_piece = w_key_value[0, 0]

    stack = [send(trunk_out, lambda m, z, k, d=d: (m, z ^ d, k)) for d in (1, 2, 3)]

    cuts = [
        lax.dynamic_slice_in_dim(query_piece, (col ^ r) * local_width, local_width, 0)
        for r in (0, 1)
    ]
    weights = [
        send(cuts[r], lambda m, z, k, r=r: (2 * k + ((m % 2) ^ r), z, m // 2))
        for r in (0, 1)
    ]

    segments, gain, kv_weight, trunk_near = prepare(
        segment_ids[None, :], norm_gain, reward_weight, kv_piece, trunk_out
    )
    column_own = stack_rows([trunk_near] + stack)
    column_other = core_swap(column_own)
    block_shape = ((tokens, block_width), bf16)
    (kv_sent,) = local_call(kv_columns_kernel, [block_shape], column_own, column_other)
    kv_got = [
        send(
            kv_sent,
            lambda m, z, k, r=r: (2 * k + ((m % 2) ^ r), z, m // 2) if m % 2 == z // 2 else None,
        )
        for r in (0, 1)
    ]
    head_shape = ((tokens, HD), f32)
    query_parts = [
        local_call(query_kernel, [head_shape], column_own, column_other, weights[r])[0]
        for r in (0, 1)
    ]
    query_got = [
        send(part, lambda m, z, k, r=r: (2 * k + ((m % 2) ^ r), z, m // 2))
        for r, part in enumerate(query_parts)
    ]
    kv_part, pooled = local_call(
        kv_kernel,
        [((tokens, 2 * HD), f32), ((SEQS, block_width), f32)],
        segments,
        *kv_got,
        kv_weight,
    )
    kv_part = kv_part + core_swap(kv_part)
    mine, swapped = height_total(kv_part, core, jnp.float16, query_got[0] + query_got[1])

    out_rows, _ = lax.optimization_barrier((w_out[0], kv_part))
    out_own = lax.dynamic_slice_in_dim(out_rows, core * half_width, half_width, 1)
    out_other = core_swap(
        lax.dynamic_slice_in_dim(out_rows, (1 - core) * half_width, half_width, 1)
    )

    queries, kv_values, attention, capped, message = local_call(
        forward_kernel,
        [
            ((tokens, HD), bf16),
            ((tokens, 2 * HD), bf16),
            ((tokens, tokens), f32),
            ((tokens, tokens), f32),
            ((SEQS, half_width + HD), bf16),
        ],
        segments, mine, swapped, pooled, out_own, out_other, gain,
    )
    others = [send(message, lambda m, z, k, d=d: (m, z ^ d, k)) for d in (1, 2, 3)]
    hidden, report = local_call(
        stats_kernel,
        [((SEQS, half_width), f32), ((3 * SEQS, HD), f32)],
        message, *others, out_own, out_other, gain,
    )
    seq_ids = jnp.arange(SEQS)[None, :]
    pairs = (pair_order[0::2][:, None] == seq_ids).astype(f32) - (
        pair_order[1::2][:, None] == seq_ids
    ).astype(f32)
    pairs = jnp.concatenate([pairs, jnp.zeros_like(pairs)], axis=0)
    query_grad, kv_grad, rewards, factors = local_call(
        functools.partial(backward_kernel, full_width=float(2 * half_width)),
        [
            ((tokens, HD), bf16),
            ((tokens, 2 * HD), f32),
            ((1, SEQS), f32),
            ((2, SEQS, HD), f32),
        ],
        pairs, segments, report, core_swap(report), queries, kv_values, attention, capped,
    )

    kv_mine, kv_swapped = height_total(kv_grad, core, bf16)
    (far_grad,) = local_call(
        far_kernel, [((tokens, 3 * block_width), bf16)], query_grad, query_piece
    )
    far_got = [
        send(far_grad[d * member_rows : (d + 1) * member_rows], lambda m, z, k, d=d: (m ^ d, z, k))
        for d in (1, 2, 3)
    ]
    (near_grad,) = local_call(
        near_kernel,
        [block_shape],
        segments, query_grad, query_piece, kv_mine, kv_swapped, kv_weight, hidden, gain,
        factors,
    )
    near_got = [
        send(near_grad[d * member_rows : (d + 1) * member_rows], lambda m, z, k, d=d: (m ^ d, z, k))
        for d in (1, 2, 3)
    ]
    sum_shape = ((member_rows, block_width), bf16)
    pair_shape = ((member_rows, 2 * block_width), bf16)
    far_one, far_pair = local_call(far_sum_kernel, [sum_shape, pair_shape], far_grad, *far_got)
    far_part = send(far_pair, lambda m, z, k: (m, 2 * k + 1 - z // 2, z % 2))
    (near_pair,) = local_call(near_sum_kernel, [pair_shape], near_grad, *near_got, far_one)
    near_part = send(near_pair, lambda m, z, k: (m, 2 * k + z // 2, z % 2))
    kept, given = local_call(
        merge_kernel,
        [((member_rows, block_width), f32), ((member_rows, block_width), bf16)],
        far_part,
        near_part,
    )
    total = kept + core_swap(given).astype(f32)
    return (total, rewards)


def solution(mesh):
    fast = dict(mesh.shape) == {"member": 4, "shard": 8}
    placed = (
        P("shard", "member"),
        P(),
        P(),
        P("member", "shard", None, None),
        P("member", "shard", None, None),
        P("member", "shard", None),
        P("member", None),
        P("member", None),
    )
    return jax.shard_map(
        fast_device if fast else general_device,
        mesh=mesh,
        in_specs=placed,
        out_specs=(P("member", "shard"), P("member", None)),
        check_vma=False,
    )
```

```python
import functools
import math

import jax
import jax.numpy as jnp
from jax import lax
from jax.experimental import pallas as pl
from jax.experimental.pallas import tpu as pltpu
from jax.sharding import PartitionSpec as P


HD = 128
SEQS = 8


KERNEL_VMEM = 8 << 20
softcap_limit = 20.0
loss_scale = 256.0
norm_eps = 1e-05


def from_partner(block, axis, stride):
    count = lax.axis_size(axis)
    route = []
    for low in range(count):
        high = low | 1 << stride
        if high != low and high < count:
            route += [(low, high), (high, low)]
    return lax.ppermute(block, axis, route)


def partner_swap(values, bit_number):
    return from_partner(values, "shard", bit_number)


def group_total(values, bit_list):
    for bit_number in bit_list:
        values = values + partner_swap(values, bit_number)
    return values


def pair_join(own_part, other_part, pair_side, join_axis):
    first_part = jnp.where(pair_side == 0, own_part, other_part)
    second_part = jnp.where(pair_side == 0, other_part, own_part)
    return jnp.concatenate([first_part, second_part], axis=join_axis)


def general_device(
    trunk_out, segment_ids, pair_order, w_query, w_key_value, w_out, norm_gain, reward_weight
):
    n_shard = lax.axis_size("shard")
    query_heads = n_shard // 2
    kv_count = max(1, query_heads // 8)
    group_size = query_heads // kv_count
    shard_index = lax.axis_index("shard")
    pair_side = shard_index % 2
    head_index = shard_index // 2
    block_index = shard_index % (2 * group_size) // 2
    local_rows, _ = trunk_out.shape
    features = lax.all_gather(trunk_out, "member", axis=1, tiled=True)
    gathered = lax.all_gather(features, "shard", axis=0, tiled=True)
    tok_count, model_width = gathered.shape
    half_width = model_width // 2
    half_rows = tok_count // 2
    half_head = HD // 2
    row_block = half_width // group_size
    scale_factor = 1.0 / math.sqrt(HD)
    group_bits = list(range((2 * group_size).bit_length() - 1))
    query_piece = w_query[0, 0]
    kv_piece = w_key_value[0, 0]
    out_rows = w_out[0]
    gain_vector = norm_gain[0]
    head_weight = reward_weight[0]
    positions = jnp.arange(tok_count)
    own_start = pair_side * half_rows
    own_positions = own_start + jnp.arange(half_rows)
    own_segments = lax.dynamic_slice_in_dim(segment_ids, own_start, half_rows, 0)
    allowed = (own_segments[:, None] == segment_ids[None, :]) & (
        positions[None, :] <= own_positions[:, None]
    )
    member_of = jnp.arange(SEQS)[:, None] == segment_ids[None, :]
    pooling = member_of.astype(jnp.bfloat16)
    lengths = jnp.sum(member_of.astype(jnp.float32), axis=1)
    own_pooling = lax.dynamic_slice_in_dim(pooling, own_start, half_rows, 1)
    half_features = lax.dynamic_slice_in_dim(gathered, pair_side * half_width, half_width, 1)
    query_partial = jnp.dot(half_features, query_piece, preferred_element_type=jnp.float32)
    kept_rows = lax.dynamic_slice_in_dim(query_partial, own_start, half_rows, 0)
    sent_rows = lax.dynamic_slice_in_dim(query_partial, half_rows - own_start, half_rows, 0)
    queries = (kept_rows + partner_swap(sent_rows, 0)).astype(jnp.bfloat16)
    kv_features = lax.dynamic_slice_in_dim(half_features, block_index * row_block, row_block, 1)
    kv_values = group_total(
        jnp.dot(kv_features, kv_piece, preferred_element_type=jnp.float32), group_bits
    ).astype(jnp.bfloat16)
    key_full = kv_values[:, :HD]
    value_full = kv_values[:, HD:]
    raw_scores = (
        jnp.einsum("td,sd->ts", queries, key_full, preferred_element_type=jnp.float32)
        * scale_factor
    )
    capped = softcap_limit * jnp.tanh(raw_scores / softcap_limit)
    weights_exp = jnp.where(allowed, jnp.exp(capped), 0.0)
    attention = weights_exp / jnp.sum(weights_exp, axis=1, keepdims=True)
    attention_low = attention.astype(jnp.bfloat16)
    attended = jnp.dot(attention_low, value_full, preferred_element_type=jnp.float32).astype(
        jnp.bfloat16
    )
    seq_part = jnp.dot(own_pooling, attended, preferred_element_type=jnp.float32)
    seq_total = seq_part + partner_swap(seq_part, 0)
    seq_mean = (seq_total / lengths[:, None]).astype(jnp.bfloat16)
    own_dims = lax.dynamic_slice_in_dim(seq_mean, pair_side * half_head, half_head, 1)
    head_part = jnp.dot(own_dims, out_rows, preferred_element_type=jnp.float32)
    pooled_attn = lax.psum(head_part, "shard")
    pooled_input = jnp.dot(pooling, gathered, preferred_element_type=jnp.float32) / lengths[:, None]
    hidden = pooled_input + pooled_attn
    inverse_rms = lax.rsqrt(jnp.mean(hidden * hidden, axis=1) + norm_eps)
    normed = hidden * inverse_rms[:, None] * gain_vector
    rewards = jnp.sum(normed * head_weight, axis=1)
    seq_ids = jnp.arange(SEQS)
    chosen = (pair_order[0::2][:, None] == seq_ids[None, :]).astype(jnp.float32)
    rejected = (pair_order[1::2][:, None] == seq_ids[None, :]).astype(jnp.float32)
    margin = jnp.sum(chosen * rewards, axis=1) - jnp.sum(rejected * rewards, axis=1)
    pair_slope = loss_scale * jax.nn.sigmoid(-margin)
    reward_grad = jnp.sum(rejected * pair_slope[:, None], axis=0) - jnp.sum(
        chosen * pair_slope[:, None], axis=0
    )
    scaled_grad = reward_grad[:, None] * head_weight * gain_vector
    hidden_grad = inverse_rms[:, None] * (
        scaled_grad
        - hidden * (inverse_rms**2)[:, None] * jnp.mean(hidden * scaled_grad, axis=1, keepdims=True)
    )
    per_token = hidden_grad / lengths[:, None]
    grad_low = hidden_grad.astype(jnp.bfloat16)
    grad_dims = (
        jnp.einsum("jd,ed->je", grad_low, out_rows, preferred_element_type=jnp.float32)
        / lengths[:, None]
    )
    mean_grad = pair_join(grad_dims, partner_swap(grad_dims, 0), pair_side, 1)
    out_grad = jnp.take(mean_grad, own_segments, axis=0).astype(jnp.bfloat16)
    prob_grad = jnp.einsum("td,sd->ts", out_grad, value_full, preferred_element_type=jnp.float32)
    score_grad = attention * (prob_grad - jnp.sum(attention * prob_grad, axis=1, keepdims=True))
    raw_grad = (score_grad * (1.0 - (capped / softcap_limit) ** 2) * scale_factor).astype(
        jnp.bfloat16
    )
    query_grad = jnp.dot(raw_grad, key_full, preferred_element_type=jnp.float32).astype(
        jnp.bfloat16
    )
    key_grad = jnp.einsum("ts,td->sd", raw_grad, queries, preferred_element_type=jnp.float32)
    value_grad = jnp.einsum(
        "ts,td->sd", attention_low, out_grad, preferred_element_type=jnp.float32
    )
    kv_grad = group_total(jnp.concatenate([key_grad, value_grad], axis=1), group_bits).astype(
        jnp.bfloat16
    )
    query_wire = lax.optimization_barrier(query_grad).astype(jnp.float32)
    query_all = pair_join(
        query_grad, partner_swap(query_wire, 0).astype(jnp.bfloat16), pair_side, 0
    )
    grad_half = jnp.einsum("td,rd->tr", query_all, query_piece, preferred_element_type=jnp.float32)
    kv_term = jnp.einsum("te,re->tr", kv_grad, kv_piece, preferred_element_type=jnp.float32)
    start_col = block_index * row_block
    grad_half = lax.dynamic_update_slice_in_dim(
        grad_half,
        lax.dynamic_slice_in_dim(grad_half, start_col, row_block, 1) + kv_term,
        start_col,
        1,
    )
    pair_rows = 2 * local_rows
    start_row = head_index * pair_rows
    pair_segments = lax.dynamic_slice_in_dim(segment_ids, start_row, pair_rows, 0)
    token_half = lax.dynamic_slice_in_dim(per_token, pair_side * half_width, half_width, 1)
    direct = jnp.take(token_half, pair_segments, axis=0)
    grad_half = lax.dynamic_update_slice_in_dim(
        grad_half,
        lax.dynamic_slice_in_dim(grad_half, start_row, pair_rows, 0) + direct,
        start_row,
        0,
    )
    by_member = lax.psum_scatter(grad_half, "member", scatter_dimension=0, tiled=True)
    member_rows = by_member.shape[0]
    placed = lax.dynamic_update_slice_in_dim(
        jnp.zeros((member_rows, model_width), jnp.float32), by_member, pair_side * half_width, 1
    )
    trunk_grad = lax.psum_scatter(placed, "shard", scatter_dimension=1, tiled=True)
    return (trunk_grad, rewards[None])


def route_pairs(target):
    pairs = []
    for member in range(4):
        for height in range(4):
            for core in range(2):
                to = target(member, height, core)
                if to is not None:
                    pairs.append((member * 8 + height * 2 + core, to[0] * 8 + to[1] * 2 + to[2]))
    return pairs


def send(block, target):
    return lax.ppermute(block, ("member", "shard"), route_pairs(target))


def core_swap(block):
    return send(block, lambda m, z, k: (m, z, 1 - k))


def matmul(left, right):
    return jnp.dot(left, right, preferred_element_type=jnp.float32)


def matmul_nt(left, right):
    return lax.dot_general(
        left, right, (((1,), (1,)), ((), ())), preferred_element_type=jnp.float32
    )


def matmul_tn(left, right):
    return lax.dot_general(
        left, right, (((0,), (0,)), ((), ())), preferred_element_type=jnp.float32
    )


def height_total(block, core, wire, beside=None):
    sent = block.astype(wire)
    near = send(sent, lambda m, z, k: (m, z ^ (1 + k), k))
    half = jnp.where(core == 0, sent[:, :HD], sent[:, HD:])
    far = send(half, lambda m, z, k: (m, z ^ 3, k)).astype(jnp.float32)
    zero = jnp.zeros_like(far)
    spread = jnp.concatenate(
        [jnp.where(core == 0, far, zero), jnp.where(core == 0, zero, far)], axis=1
    )
    mine = jnp.where(core == 0, sent.astype(jnp.float32), 0.0) + near.astype(jnp.float32) + spread
    if beside is not None:
        mine = jnp.concatenate([mine, beside], axis=1)
    return mine, core_swap(mine)


def split_high_low(value):
    high = value.astype(jnp.bfloat16)
    return high, (value - high.astype(jnp.float32)).astype(jnp.bfloat16)


def iota(shape, dimension):
    return lax.broadcasted_iota(jnp.int32, shape, dimension)


def one_hot(condition):
    return condition.astype(jnp.float32).astype(jnp.bfloat16)


def pooling_of(segments):
    return one_hot(iota((SEQS, segments.shape[1]), 0) == segments)


def lengths_of(segments):
    return jnp.sum(
        (iota((SEQS, segments.shape[1]), 0) == segments).astype(jnp.float32), axis=1, keepdims=True
    )


def here():
    return lax.axis_index("member"), lax.axis_index("shard")


def local_call(kernel, outputs, *operands):
    vmem = pl.BlockSpec(memory_space=pltpu.VMEM)
    return pl.pallas_call(
        kernel,
        out_shape=[jax.ShapeDtypeStruct(shape, dtype) for shape, dtype in outputs],
        in_specs=[vmem] * len(operands),
        out_specs=[vmem] * len(outputs),
        compiler_params=pltpu.CompilerParams(vmem_limit_bytes=KERNEL_VMEM),
    )(*operands)


def prepare_kernel(
    segment_ids, norm_gain, reward_weight, weight, trunk,
    segments_out, gain_out, weight_out, trunk_out, head_weight, sems,
):
    place = here()
    width = gain_out.shape[1]
    start = pl.multiple_of(place[1] % 2 * width, width)
    copies = [
        pltpu.make_async_copy(weight, weight_out, sems.at[0]),
        pltpu.make_async_copy(segment_ids, segments_out, sems.at[1]),
        pltpu.make_async_copy(norm_gain.at[:, pl.ds(start, width)], gain_out, sems.at[2]),
        pltpu.make_async_copy(reward_weight.at[:, pl.ds(start, width)], head_weight, sems.at[3]),
        pltpu.make_async_copy(trunk, trunk_out, sems.at[4]),
    ]
    for copy in copies:
        copy.start()
    for copy in copies:
        copy.wait()
    gain_out[...] = gain_out[...] * head_weight[...]


def prepare(segments, norm_gain, reward_weight, weight, trunk):
    width = norm_gain.shape[1] // 2
    return pl.pallas_call(
        prepare_kernel,
        out_shape=[
            jax.ShapeDtypeStruct(segments.shape, segments.dtype),
            jax.ShapeDtypeStruct((1, width), norm_gain.dtype),
            jax.ShapeDtypeStruct(weight.shape, weight.dtype),
            jax.ShapeDtypeStruct(trunk.shape, trunk.dtype),
        ],
        in_specs=[pl.BlockSpec(memory_space=pl.ANY)] * 5,
        out_specs=[pl.BlockSpec(memory_space=pltpu.VMEM)] * 4,
        scratch_shapes=[
            pltpu.VMEM((1, width), reward_weight.dtype),
            pltpu.SemaphoreType.DMA((5,)),
        ],
        compiler_params=pltpu.CompilerParams(vmem_limit_bytes=KERNEL_VMEM),
    )(segments, norm_gain, reward_weight, weight, trunk)


def stack_kernel(*refs):
    place = here()
    pieces, out, sems = refs[:-2], refs[-2], refs[-1]
    rows = pieces[0].shape[0]
    copies = []
    for step, ref in enumerate(pieces):
        start = pl.multiple_of(((place[1] // 2) ^ step) * rows, rows)
        copies.append(pltpu.make_async_copy(ref, out.at[pl.ds(start, rows), :], sems.at[step]))
    for copy in copies:
        copy.start()
    for copy in copies:
        copy.wait()


def stack_rows(blocks):
    rows, width = blocks[0].shape
    return pl.pallas_call(
        stack_kernel,
        out_shape=jax.ShapeDtypeStruct((len(blocks) * rows, width), blocks[0].dtype),
        in_specs=[pl.BlockSpec(memory_space=pl.ANY)] * len(blocks),
        out_specs=pl.BlockSpec(memory_space=pltpu.VMEM),
        scratch_shapes=[pltpu.SemaphoreType.DMA((len(blocks),))],
        compiler_params=pltpu.CompilerParams(vmem_limit_bytes=KERNEL_VMEM),
    )(*blocks)


def kv_columns_kernel(own, other, out):
    place = here()
    width = out.shape[1]
    rows = own.shape[0] // 4
    core = place[1] % 2
    start = pl.multiple_of(place[1] // 2 % 2 * width, width)
    for source, side in ((own, core), (other, 1 - core)):
        for step in range(4):
            to = pl.multiple_of((2 * step + side) * rows, rows)
            out[pl.ds(to, rows), :] = source[step * rows : (step + 1) * rows, pl.ds(start, width)]


def query_kernel(own, other, weight, out):
    place = here()
    rows = own.shape[0] // 4
    core = place[1] % 2
    for source, side in ((own, core), (other, 1 - core)):
        part = matmul(source[...], weight[...])
        for step in range(4):
            to = pl.multiple_of((2 * step + side) * rows, rows)
            out[pl.ds(to, rows), :] = part[step * rows : (step + 1) * rows]


def kv_kernel(segments, first, second, weight, out, pooled):
    place = here()
    far = (place[1] // 4) ^ (place[0] % 2)
    columns = jnp.where(far == 0, first[...], second[...])
    out[...] = matmul(columns, weight[...])
    pooled[...] = matmul(pooling_of(segments[...]), columns) / lengths_of(segments[...])


def forward_kernel(
    segments, mine, swapped, pooled, out_own, out_other, gain,
    queries_out, kv_out, attention_out, capped_out, message,
):
    bf16 = jnp.bfloat16
    place = here()
    core, height = place[1] % 2, place[1] // 2
    queries = (mine[:, 2 * HD :] + swapped[:, 2 * HD :]).astype(bf16)
    kv_values = (mine[:, : 2 * HD] + swapped[:, : 2 * HD]).astype(bf16)
    queries_out[...] = queries
    kv_out[...] = kv_values
    keys, values = kv_values[:, :HD], kv_values[:, HD:]
    pooling = pooling_of(segments[...])
    lengths = lengths_of(segments[...])
    tokens = pooling.shape[1]
    same = matmul_tn(pooling, pooling) > 0.5
    allowed = same & (iota((tokens, tokens), 1) <= iota((tokens, tokens), 0))
    raw_scores = matmul_nt(queries, keys) * (1.0 / math.sqrt(HD))
    capped = softcap_limit * jnp.tanh(raw_scores / softcap_limit)
    weights_exp = jnp.where(allowed, jnp.exp(capped), 0.0)
    attention = weights_exp / jnp.sum(weights_exp, axis=1, keepdims=True)
    attention_out[...] = attention
    capped_out[...] = capped
    attended = matmul(attention.astype(bf16), values).astype(bf16)
    seq_mean = (matmul(pooling, attended) / lengths).astype(bf16)
    half = out_own.shape[0]
    low, high = seq_mean[:, :half], seq_mean[:, half:]
    part = matmul(jnp.where(core == 0, low, high), out_own[...]) + matmul(
        jnp.where(core == 0, high, low), out_other[...]
    )
    width = pooled.shape[1]
    part = jnp.concatenate(
        [
            part[:, n * width : (n + 1) * width] + jnp.where(height == n, pooled[...], 0.0)
            for n in range(part.shape[1] // width)
        ],
        axis=1,
    )
    product_high, product_low = split_high_low(jnp.sum(part * gain[...], axis=1, keepdims=True))
    lane = iota((SEQS, HD), 1)
    message[:, : part.shape[1]] = part.astype(bf16)
    message[:, part.shape[1] :] = jnp.where(
        lane == 0,
        product_high.astype(jnp.float32),
        jnp.where(lane == 1, product_low.astype(jnp.float32), 0.0),
    ).astype(bf16)


def stats_kernel(
    first, second, third, fourth, out_own, out_other, gain, hidden_out, report
):
    core = here()[1] % 2
    half_width = hidden_out.shape[1]
    f32 = jnp.float32
    total = (first[...].astype(f32) + second[...].astype(f32)) + (
        third[...].astype(f32) + fourth[...].astype(f32)
    )
    hidden = total[:, :half_width]
    hidden_out[...] = hidden
    stacked = jnp.concatenate([hidden, jnp.broadcast_to(gain[...], hidden.shape)], axis=0)
    stacked = stacked.astype(jnp.bfloat16)
    along_own = matmul_nt(stacked, out_own[...])
    along_other = matmul_nt(stacked, out_other[...])
    half = along_own.shape[1]
    report[: 2 * SEQS, :half] = jnp.where(core == 0, along_own, along_other)
    report[: 2 * SEQS, half:] = jnp.where(core == 0, along_other, along_own)
    squares = jnp.sum(hidden * hidden, axis=1, keepdims=True)
    products = total[:, half_width : half_width + 1] + total[:, half_width + 1 : half_width + 2]
    lane = iota((SEQS, HD), 1)
    report[2 * SEQS :, :] = jnp.where(lane == 0, squares, jnp.where(lane == 1, products, 0.0))


def member_order(place, tokens):
    rows = tokens // 4
    position = iota((tokens, tokens), 0)
    token = rows * (place[0] ^ (position // rows)) + position % rows
    return one_hot(iota((tokens, tokens), 1) == token)


def backward_kernel(
    pairs, segments, mine, swapped, queries, kv_values, attention, capped,
    weight, query_grad, kv_grad, rewards_out, factors, far, *, full_width,
):
    bf16 = jnp.bfloat16
    width = full_width
    report = mine[...] + swapped[...]
    hidden_along, gain_along = report[:SEQS], report[SEQS : 2 * SEQS]
    square_sum, product_sum = report[2 * SEQS :, 0:1], report[2 * SEQS :, 1:2]
    pooling = pooling_of(segments[...])
    lengths = lengths_of(segments[...])
    inverse_rms = lax.rsqrt(square_sum / width + norm_eps)
    rewards = product_sum * inverse_rms
    diagonal = iota((SEQS, SEQS), 0) == iota((SEQS, SEQS), 1)
    rewards_row = jnp.sum(jnp.where(diagonal, rewards, 0.0), axis=0, keepdims=True)
    rewards_out[...] = rewards_row
    signs = pairs[...]
    margin = jnp.sum(signs * rewards_row, axis=1, keepdims=True)
    pair_slope = loss_scale / (1.0 + jnp.exp(margin))
    grad_row = -jnp.sum(signs * pair_slope, axis=0, keepdims=True)
    reward_grad = jnp.sum(jnp.where(diagonal, grad_row, 0.0), axis=1, keepdims=True)
    gain_factor = inverse_rms * reward_grad / lengths
    hidden_factor = inverse_rms * inverse_rms * inverse_rms * (
        reward_grad * product_sum / width
    ) / lengths
    factors[0] = jnp.broadcast_to(gain_factor, (SEQS, HD))
    factors[1] = jnp.broadcast_to(hidden_factor, (SEQS, HD))
    mean_grad = (gain_factor * gain_along - hidden_factor * hidden_along).astype(bf16)
    out_grad = matmul_tn(pooling, mean_grad).astype(bf16)
    keys, values = kv_values[:, :HD], kv_values[:, HD:]
    attn = attention[...]
    prob_grad = matmul_nt(out_grad, values)
    score_grad = attn * (prob_grad - jnp.sum(attn * prob_grad, axis=1, keepdims=True))
    ratio = capped[...] / softcap_limit
    raw_grad = (score_grad * (1.0 - ratio * ratio) * (1.0 / math.sqrt(HD))).astype(bf16)
    order = member_order(here(), attn.shape[0])
    turned = matmul(order, matmul(raw_grad, keys).astype(bf16)).astype(bf16)
    query_grad[...] = turned
    block = far.shape[1] // 3
    for step in (1, 2, 3):
        start = pl.multiple_of(((here()[1] // 2) ^ step) * block, block)
        far[:, (step - 1) * block : step * block] = matmul_nt(
            turned, weight[pl.ds(start, block), :]
        ).astype(far.dtype)
    kv_grad[:, :HD] = matmul_tn(raw_grad, queries[...])
    kv_grad[:, HD:] = matmul_tn(attn.astype(bf16), out_grad)


def near_kernel(
    segments, grad, weight, kv_mine, kv_swapped, kv_weight, hidden, gain, factors, near
):
    bf16 = jnp.bfloat16
    place = here()
    width = near.shape[1]
    start = pl.multiple_of(place[1] // 2 * width, width)
    order = member_order(place, near.shape[0])
    kv_grad = (kv_mine[...] + kv_swapped[...]).astype(bf16)
    kv_turned = matmul(order, kv_grad).astype(bf16)
    seq_turned = matmul_nt(order, pooling_of(segments[...])).astype(bf16)
    gain_block = gain[:, pl.ds(start, width)]
    high, low = split_high_low(
        factors[0][:, 0:1] * gain_block - factors[1][:, 0:1] * hidden[:, pl.ds(start, width)]
    )
    near[...] = (
        matmul_nt(grad[...], weight[pl.ds(start, width), :])
        + matmul_nt(kv_turned, kv_weight[...])
        + matmul(seq_turned, high)
        + matmul(seq_turned, low)
    ).astype(bf16)


def sum_of(own, first, second, third, start, width):
    f32 = jnp.float32
    rows = first.shape[0]
    return (
        (own[:rows, start : start + width].astype(f32) + first[:, start : start + width].astype(f32))
        + (
            second[:, start : start + width].astype(f32)
            + third[:, start : start + width].astype(f32)
        )
    ).astype(own.dtype)


def place_of(step, width):
    return pl.multiple_of(((here()[1] // 2) ^ step) % 2 * width, width)


def far_sum_kernel(own, first, second, third, one, two):
    width = one.shape[1]
    one[...] = sum_of(own, first, second, third, 0, width)
    for step in (2, 3):
        two[:, pl.ds(place_of(step, width), width)] = sum_of(
            own, first, second, third, (step - 1) * width, width
        )


def near_sum_kernel(own, first, second, third, one, two):
    width = one.shape[1]
    two[:, pl.ds(place_of(0, width), width)] = sum_of(own, first, second, third, 0, width)
    two[:, pl.ds(place_of(1, width), width)] = one[...]


def merge_kernel(first, second, kept, given):
    width = kept.shape[1]
    core = here()[1] % 2
    for out, side in ((kept, core), (given, 1 - core)):
        columns = pl.ds(pl.multiple_of(side * width, width), width)
        out[...] = (
            first[:, columns].astype(jnp.float32) + second[:, columns].astype(jnp.float32)
        ).astype(out.dtype)


def fast_device(
    trunk_out, segment_ids, pair_order, w_query, w_key_value, w_out, norm_gain, reward_weight
):
    bf16, f32 = jnp.bfloat16, jnp.float32
    member = lax.axis_index("member")
    shard = lax.axis_index("shard")
    core = shard % 2
    col = member % 2
    local_width = trunk_out.shape[1]
    tokens = segment_ids.shape[0]
    half_width = w_query.shape[2]
    block_width = w_key_value.shape[2]
    member_rows = tokens // 4
    query_piece = w_query[0, 0]
    kv_piece = w_key_value[0, 0]

    stack = [send(trunk_out, lambda m, z, k, d=d: (m, z ^ d, k)) for d in (1, 2, 3)]

    cuts = [
        lax.dynamic_slice_in_dim(query_piece, (col ^ r) * local_width, local_width, 0)
        for r in (0, 1)
    ]
    weights = [
        send(cuts[r], lambda m, z, k, r=r: (2 * k + ((m % 2) ^ r), z, m // 2))
        for r in (0, 1)
    ]

    segments, gain, kv_weight, trunk_near = prepare(
        segment_ids[None, :], norm_gain, reward_weight, kv_piece, trunk_out
    )
    column_own = stack_rows([trunk_near] + stack)
    column_other = core_swap(column_own)
    block_shape = ((tokens, block_width), bf16)
    (kv_sent,) = local_call(kv_columns_kernel, [block_shape], column_own, column_other)
    kv_got = [
        send(
            kv_sent,
            lambda m, z, k, r=r: (2 * k + ((m % 2) ^ r), z, m // 2) if m % 2 == z // 2 else None,
        )
        for r in (0, 1)
    ]
    head_shape = ((tokens, HD), f32)
    query_parts = [
        local_call(query_kernel, [head_shape], column_own, column_other, weights[r])[0]
        for r in (0, 1)
    ]
    query_got = [
        send(part, lambda m, z, k, r=r: (2 * k + ((m % 2) ^ r), z, m // 2))
        for r, part in enumerate(query_parts)
    ]
    kv_part, pooled = local_call(
        kv_kernel,
        [((tokens, 2 * HD), f32), ((SEQS, block_width), f32)],
        segments,
        *kv_got,
        kv_weight,
    )
    kv_part = kv_part + core_swap(kv_part)
    mine, swapped = height_total(kv_part, core, jnp.float16, query_got[0] + query_got[1])

    out_rows, _ = lax.optimization_barrier((w_out[0], kv_part))
    out_own = lax.dynamic_slice_in_dim(out_rows, core * half_width, half_width, 1)
    out_other = core_swap(
        lax.dynamic_slice_in_dim(out_rows, (1 - core) * half_width, half_width, 1)
    )

    queries, kv_values, attention, capped, message = local_call(
        forward_kernel,
        [
            ((tokens, HD), bf16),
            ((tokens, 2 * HD), bf16),
            ((tokens, tokens), f32),
            ((tokens, tokens), f32),
            ((SEQS, half_width + HD), bf16),
        ],
        segments, mine, swapped, pooled, out_own, out_other, gain,
    )
    others = [send(message, lambda m, z, k, d=d: (m, z ^ d, k)) for d in (1, 2, 3)]
    hidden, report = local_call(
        stats_kernel,
        [((SEQS, half_width), f32), ((3 * SEQS, HD), f32)],
        message, *others, out_own, out_other, gain,
    )
    seq_ids = jnp.arange(SEQS)[None, :]
    pairs = (pair_order[0::2][:, None] == seq_ids).astype(f32) - (
        pair_order[1::2][:, None] == seq_ids
    ).astype(f32)
    pairs = jnp.concatenate([pairs, jnp.zeros_like(pairs)], axis=0)
    query_grad, kv_grad, rewards, factors, far_grad = local_call(
        functools.partial(backward_kernel, full_width=float(2 * half_width)),
        [
            ((tokens, HD), bf16),
            ((tokens, 2 * HD), f32),
            ((1, SEQS), f32),
            ((2, SEQS, HD), f32),
            ((tokens, 3 * block_width), bf16),
        ],
        pairs, segments, report, core_swap(report), queries, kv_values, attention, capped,
        query_piece,
    )

    kv_mine, kv_swapped = height_total(kv_grad, core, bf16)
    far_got = [
        send(far_grad[d * member_rows : (d + 1) * member_rows], lambda m, z, k, d=d: (m ^ d, z, k))
        for d in (1, 2, 3)
    ]
    (near_grad,) = local_call(
        near_kernel,
        [block_shape],
        segments, query_grad, query_piece, kv_mine, kv_swapped, kv_weight, hidden, gain,
        factors,
    )
    near_got = [
        send(near_grad[d * member_rows : (d + 1) * member_rows], lambda m, z, k, d=d: (m ^ d, z, k))
        for d in (1, 2, 3)
    ]
    sum_shape = ((member_rows, block_width), bf16)
    pair_shape = ((member_rows, 2 * block_width), bf16)
    far_one, far_pair = local_call(far_sum_kernel, [sum_shape, pair_shape], far_grad, *far_got)
    far_part = send(far_pair, lambda m, z, k: (m, 2 * k + 1 - z // 2, z % 2))
    (near_pair,) = local_call(near_sum_kernel, [pair_shape], near_grad, *near_got, far_one)
    near_part = send(near_pair, lambda m, z, k: (m, 2 * k + z // 2, z % 2))
    kept, given = local_call(
        merge_kernel,
        [((member_rows, block_width), f32), ((member_rows, block_width), bf16)],
        far_part,
        near_part,
    )
    total = kept + core_swap(given).astype(f32)
    return (total, rewards)


def solution(mesh):
    fast = dict(mesh.shape) == {"member": 4, "shard": 8}
    placed = (
        P("shard", "member"),
        P(),
        P(),
        P("member", "shard", None, None),
        P("member", "shard", None, None),
        P("member", "shard", None),
        P("member", None),
        P("member", None),
    )
    return jax.shard_map(
        fast_device if fast else general_device,
        mesh=mesh,
        in_specs=placed,
        out_specs=(P("member", "shard"), P("member", None)),
        check_vma=False,
    )
```
